128 devices in a mesh: ty: 8 (over y, core), tx: 16 (over x, z).
Axes of the slice: x: 4, y: 4, z: 4, core: 2. Of those that a mesh axis runs over, the one named last changes fastest.
Arguments:
- source_fields: float32 [8, 768, 4096], P(None, 'ty', 'tx'), may hold values from -6 to 6
- diffusivity: float32 [768, 4096], P('ty', 'tx'), may hold values from 0.03 to 0.24
- cell_area: float32 [768, 4096], P('ty', 'tx'), may hold values from 0.5 to 2
- pair_block: int32 [32768], P(('ty', 'tx')), may hold values from 0 to 191
- pair_owner: int32 [32768, 1], P(('ty', 'tx')), may hold values from 0 to 127; in each aligned block of 256 rows (0 to 255, 256 to 511, ...) at most 4 rows name the same one
- pair_target: int32 [32768], P(('ty', 'tx')), may hold values from 0 to 15
- weight_blocks: bfloat16 [32768, 128, 128], P(('ty', 'tx')), may hold values from 0.0099487305 to 0.099609375
- target_area: float32 [2048, 128], P(('ty', 'tx')), may hold values from 1 to 4
Outputs:
- regridded: float32 [2048, 8, 128], P(('ty', 'tx'))
The draws below stay inside these ranges and needn't reach their ends.
Inputs may be any that keep to these rules, and one draw needn't show every extreme that they name: `pair_owner`: among the 256 pairs held by one device, no owner is named more than 4 times; some device names some owner exactly 4 times.
All inputs are finite; a program needn't handle non-finite values.
Results may differ from the reference program's by a relative error of at most 0.0018.
Values sent between devices are 32-bit elements; how exact they have to be, the bound alone decides.
A program may use at most 64 MiB of HBM per device.

```python
import math
import jax
import jax.numpy as jnp
import numpy as np
from jax import lax

NVAR = 8
BH = 8
BW = 16
BR = 12
BCOL = 16
TBD = 16
PAIRS = 256
CAP = 4
SRC_R = 768
SRC_C = 4096
NTGT = 2048
NPAIR = 32768
N_TY = 8
N_TX = 16
DEVICES = 128


def touch_ends(values, stream_key, low, high):
    place = [jax.random.randint(jax.random.fold_in(stream_key, axis), (), 0, length) for axis, length in enumerate(values.shape)]
    widest = values.shape.index(max(values.shape))
    beside = place[:widest] + [(place[widest] + 1) % values.shape[widest]] + place[widest + 1:]
    return values.at[tuple(place)].set(low).at[tuple(beside)].set(high)


def steps_of(rng, shape, split, low, high):
    loudness, own = 1.0, jax.random.fold_in(rng, 6)
    for position, shards_of in split:
        steps = jnp.exp(jax.random.uniform(jax.random.fold_in(own, position), (shards_of,), jnp.float32, low / len(split), high / len(split)))
        loudness = loudness * jnp.repeat(steps, shape[position] // shards_of).reshape([-1 if axis == position else 1 for axis in range(len(shape))])
    return loudness


def deal_out(stream_key, own, number, rows, number_of, top, limit, lean):
    order = jax.random.permutation(stream_key, number_of)
    heavy_load, usual = portions_of(number_of, rows * top, limit, lean, True), portions_of(number_of, rows * top, limit, lean, False)
    places = jnp.arange(number_of)

    def named(lengths, turn):
        used = int((lengths > 0).sum())
        fixed = max(1, used // 4)
        passed = fixed + (places - fixed + turn * (used - fixed)) % max(1, number_of - fixed)
        return jnp.zeros((number_of,), jnp.int32).at[order[jnp.where(places < fixed, places, passed)]].set(jnp.asarray(lengths, jnp.int32))

    lengths = jnp.where(number % 4 == 0, named(heavy_load, number // 4), named(usual, number - number // 4 - 1))
    mixed = jax.random.permutation(jax.random.fold_in(own, 3), number_of)
    giver, sink = mixed[0:number_of // 2 * 2:2], mixed[1:number_of // 2 * 2:2]
    slack = jnp.minimum(lengths[giver] - 1, limit - lengths[sink]) // 2
    slack = jnp.where((giver == order[0]) | (sink == order[0]) | (lengths[sink] == 0), 0, jnp.maximum(slack, 0))
    passed = jax.random.randint(jax.random.fold_in(own, 4), (number_of // 2,), 0, 1 << 20) % (slack + 1)
    lengths = lengths.at[giver].add(-passed).at[sink].add(passed)
    labels = jnp.searchsorted(jnp.cumsum(lengths), jnp.arange(rows * top), side="right").astype(jnp.int32)
    listing = labels.reshape(top, rows).T
    listing = listing[jax.random.permutation(jax.random.fold_in(own, 1), rows)]
    turn = jax.random.randint(jax.random.fold_in(own, 2), (rows, 1), 0, top)
    return jnp.take_along_axis(listing, (jnp.arange(top)[None, :] + turn) % top, axis=1)


def portions_of(count, total, bound, lean, full):
    loads = [(1 << 20) // math.isqrt(grade ** lean) + 1 for grade in range(1, count + 1)]
    largest = bound if full else min(bound, max(-(-total // count), total * loads[0] // sum(loads)))
    least = 1 if total - largest >= count - 1 else 0
    counts, rest = [largest] + [least] * (count - 1), total - largest - least * (count - 1)
    while rest > 0:
        free = [i for i in range(1, count) if counts[i] < largest] or [i for i in range(1, count) if counts[i] < bound]
        mass, budget = sum([loads[i] for i in free]), rest
        for i in free:
            more = min(bound - counts[i], max(1, budget * loads[i] // mass), rest)
            counts[i] = counts[i] + more
            rest = rest - more
    return np.array(counts)


def scatter_about(stream_key, shape, scale, bound, shards=(), kind=jnp.bfloat16):
    result = scale * jax.random.normal(stream_key, shape, jnp.float32)
    if shards:
        result = result * steps_of(stream_key, shape, shards, -0.22, 0.18)
    return jnp.clip(result, -bound, bound).astype(kind)


def setup_inputs(seed: int = 0) -> dict:
    seeds = jax.random.split(jax.random.key(seed), 9)
    source_fields = scatter_about(seeds[0], (NVAR, SRC_R, SRC_C), 1.0, 6.0, ((1, 8), (2, 16)), jnp.float32)
    diffusivity = jnp.clip(jnp.exp(math.log(0.24) - 2.0794415 * jax.random.uniform(seeds[1], (SRC_R, SRC_C), jnp.float32) ** steps_of(seeds[1], (SRC_R, SRC_C), ((0, 8), (1, 16)), -0.2, 0.2)), 0.03, 0.24)
    cell_area = jnp.clip(jnp.exp(math.log(2.0) - 1.3862944 * jax.random.uniform(seeds[2], (SRC_R, SRC_C), jnp.float32) ** steps_of(seeds[2], (SRC_R, SRC_C), ((0, 8), (1, 16)), -0.2, 0.2)), 0.5, 2.0)
    pair_block = touch_ends(jax.random.randint(seeds[3], (NPAIR,), 0, BR * BCOL), jax.random.fold_in(seeds[3], 1), 0, (BR * BCOL) - 1).astype(jnp.int32)
    pair_owner_keys = jax.random.split(jax.random.fold_in(seeds[4], 1), NPAIR // PAIRS)
    pair_owner_turns = jax.random.permutation(jax.random.fold_in(seeds[4], 3), NPAIR // PAIRS)
    pair_owner = jax.vmap(lambda own, number: deal_out(jax.random.fold_in(seeds[4], 2), own, number, PAIRS, DEVICES, 1, CAP, 2))(pair_owner_keys, pair_owner_turns).reshape((NPAIR, 1))
    pair_target = touch_ends(jax.random.randint(seeds[5], (NPAIR,), 0, TBD), jax.random.fold_in(seeds[5], 1), 0, TBD - 1).astype(jnp.int32)
    weight_blocks = jnp.clip(jnp.exp(math.log(0.099609375) - 2.3038113 * jax.random.uniform(seeds[6], (NPAIR, BH * BW, BH * BW), jnp.float32) ** steps_of(seeds[6], (NPAIR, BH * BW, BH * BW), ((0, 128),), -0.2, 0.2)), 0.0099487305, 0.099609375).astype(jnp.bfloat16)
    target_area = jnp.clip(jnp.exp(math.log(4.0) - 1.3862944 * jax.random.uniform(seeds[7], (NTGT, BH * BW), jnp.float32) ** steps_of(seeds[7], (NTGT, BH * BW), ((0, 128),), -0.2, 0.2)), 1.0, 4.0)
    return dict(source_fields=source_fields, diffusivity=diffusivity, cell_area=cell_area, pair_block=pair_block, pair_owner=pair_owner, pair_target=pair_target, weight_blocks=weight_blocks, target_area=target_area)


def diffuse(values, rates):
    row_count = values.shape[1]
    eastern = jnp.roll(values, -1, axis=2)
    western = jnp.roll(values, 1, axis=2)
    k_east = 0.5 * (rates + jnp.roll(rates, -1, axis=1))
    k_west = 0.5 * (rates + jnp.roll(rates, 1, axis=1))
    zero_values = jnp.zeros_like(values[:, :1])
    northern = jnp.concatenate([values[:, 1:], zero_values], axis=1)
    southern = jnp.concatenate([zero_values, values[:, :-1]], axis=1)
    zero_rates = jnp.zeros_like(rates[:1])
    k_north = 0.5 * (rates + jnp.concatenate([rates[1:], zero_rates], axis=0))
    k_south = 0.5 * (rates + jnp.concatenate([zero_rates, rates[:-1]], axis=0))
    row_index = jnp.arange(row_count, dtype=jnp.int32)[:, None]
    k_north = jnp.where(row_index < row_count - 1, k_north, 0.0)
    k_south = jnp.where(row_index > 0, k_south, 0.0)
    return (values + k_east * (eastern - values) + k_west * (western - values)
            + k_north * (northern - values) + k_south * (southern - values))


def product(operands):
    sources, weights = operands
    return jnp.einsum("pvc,pcd->pvd", sources.astype(jnp.float32), weights.astype(jnp.float32))


def reference(source_fields, diffusivity, cell_area, pair_block, pair_owner, pair_target, weight_blocks, target_area):
    smoothed = diffuse(diffuse(source_fields, diffusivity), diffusivity)
    scaled = (cell_area[None] * smoothed).astype(jnp.bfloat16)
    device_count = N_TY * N_TX
    shaped = scaled.reshape(NVAR, N_TY, BR, BH, N_TX, BCOL, BW)
    blocks = shaped.transpose(1, 4, 2, 5, 0, 3, 6).reshape(device_count * BR * BCOL, NVAR, BH * BW)
    offsets = (jnp.arange(device_count * PAIRS, dtype=jnp.int32) // PAIRS) * (BR * BCOL)
    chosen = blocks[(offsets + pair_block).astype(jnp.int32)]
    partials = lax.map(product, (chosen.reshape(device_count, PAIRS, NVAR, BH * BW),
                                 weight_blocks.reshape(device_count, PAIRS, BH * BW, BH * BW)))
    target_rows = (pair_owner[:, 0] * TBD + pair_target).astype(jnp.int32)
    summed = jax.ops.segment_sum(partials.reshape(device_count * PAIRS, NVAR, BH * BW), target_rows,
                                 num_segments=device_count * TBD)
    return summed / target_area[:, None, :]
```

```python
import functools

import jax
import jax.numpy as jnp
from jax import lax
from jax.experimental import pallas as pl
from jax.experimental.pallas import tpu as pltpu
from jax.sharding import PartitionSpec as P

NVAR = 8
BH = 8
BW = 16
BR = 12
BCOL = 16
TBD = 16
CAP = 4
MESH = pl.DeviceIdType.MESH
STEP, BACK = 51, 123


def padded_2(shard, sides, width):
    for axis, dim in sides:
        peers, length = (lax.axis_size(axis), shard.shape[dim])
        up = [(i, (i + 1) % peers) for i in range(peers)]
        down = [(j, i) for i, j in up]
        last = lax.slice_in_dim(shard, length - width, length, axis=dim)
        initial = lax.slice_in_dim(shard, 0, width, axis=dim)
        before = lax.ppermute(last, axis, up)
        after = lax.ppermute(initial, axis, down)
        shard = jnp.concatenate([before, shard, after], axis=dim)
    return shard


def diffuse(padded, rate_padded, row_start, total_rows):
    centre = padded[:, 1:-1, 1:-1]
    own_rate = rate_padded[1:-1, 1:-1]
    k_east = 0.5 * (own_rate + rate_padded[1:-1, 2:])
    k_west = 0.5 * (own_rate + rate_padded[1:-1, :-2])
    k_north = 0.5 * (own_rate + rate_padded[2:, 1:-1])
    k_south = 0.5 * (own_rate + rate_padded[:-2, 1:-1])
    row_index = row_start + lax.iota(jnp.int32, centre.shape[1])[:, None]
    k_north = jnp.where(row_index < total_rows - 1, k_north, 0.0)
    k_south = jnp.where(row_index > 0, k_south, 0.0)
    return (
        centre
        + k_east * (padded[:, 1:-1, 2:] - centre)
        + k_west * (padded[:, 1:-1, :-2] - centre)
        + k_north * (padded[:, 2:, 1:-1] - centre)
        + k_south * (padded[:, :-2, 1:-1] - centre)
    )


def barrier(ny, nx, second):
    ty, tx = lax.axis_index("ty"), lax.axis_index("tx")
    first = pltpu.get_barrier_semaphore()
    for d in range(1, nx):
        pl.semaphore_signal(first, inc=1, device_id=(ty, lax.rem(tx + d, nx)), device_id_type=MESH)
    for d in range(1, ny):
        pl.semaphore_signal(first, inc=1, device_id=(lax.rem(ty + d, ny), tx), device_id_type=MESH)
    pl.semaphore_wait(first, nx - 1 + ny - 1)
    for d in range(1, ny):
        pl.semaphore_signal(second, inc=1, device_id=(lax.rem(ty + d, ny), tx), device_id_type=MESH)
    pl.semaphore_wait(second, ny - 1)


def exchange_kernel(
    ny, nx, send_ref, meta_ref, area_ref, out_ref,
    got, meta_got, meta_smem, send_sem, recv_sem, meta_send_sem, meta_recv_sem, local_sem, ready,
):
    n = ny * nx
    me = lax.axis_index("ty") * nx + lax.axis_index("tx")
    barrier(ny, nx, ready)

    def to(d):
        peer = lax.rem(me + lax.rem(d * STEP, n), n)
        return (peer // nx, lax.rem(peer, nx))

    def meta_copy(d):
        return pltpu.make_async_remote_copy(
            src_ref=meta_ref.at[d], dst_ref=meta_got.at[d], send_sem=meta_send_sem.at[d],
            recv_sem=meta_recv_sem.at[d], device_id=to(d), device_id_type=MESH)

    def data_copy(d):
        return pltpu.make_async_remote_copy(
            src_ref=send_ref.at[d], dst_ref=got.at[d], send_sem=send_sem.at[d],
            recv_sem=recv_sem.at[d], device_id=to(d), device_id_type=MESH)

    def start(copy):
        def body(d, carry):
            copy(d).start()
            return carry
        lax.fori_loop(1, n, body, 0)

    def finish(copy):
        def body(d, carry):
            copy(d).wait()
            return carry
        lax.fori_loop(1, n, body, 0)

    start(meta_copy)
    start(data_copy)
    meta_got[0] = meta_ref[0]
    got[0] = send_ref[0]
    finish(meta_copy)
    table = pltpu.make_async_copy(meta_got, meta_smem, local_sem)
    table.start()
    table.wait()

    def add(d, sums):
        sums = list(sums)
        for k in range(CAP):
            tile = got[d, k]
            t = meta_smem[d, 0, k]
            for j in range(TBD):
                sums[j] = sums[j] + jnp.where(t == j, tile, 0.0)
        return tuple(sums)

    def body(d, sums):
        data_copy(d).wait()
        return add(d, sums)

    zero = jnp.zeros((NVAR, BH * BW), jnp.float32)
    sums = add(0, (zero,) * TBD)
    sums = lax.fori_loop(1, n, body, sums)
    for j in range(TBD):
        out_ref[j] = sums[j] / area_ref[pl.ds(j, 1), :]


def exchange(ny, nx, send, meta, area):
    n = ny * nx
    vmem = pl.BlockSpec(memory_space=pltpu.VMEM)
    return pl.pallas_call(
        functools.partial(exchange_kernel, ny, nx),
        out_shape=jax.ShapeDtypeStruct((TBD, NVAR, BH * BW), jnp.float32),
        in_specs=[vmem, vmem, vmem],
        out_specs=vmem,
        scratch_shapes=[
            pltpu.VMEM((n, CAP, NVAR, BH * BW), jnp.float32),
            pltpu.VMEM((n, 1, 128), jnp.int32),
            pltpu.SMEM((n, 1, 128), jnp.int32),
            pltpu.SemaphoreType.DMA((n,)),
            pltpu.SemaphoreType.DMA((n,)),
            pltpu.SemaphoreType.DMA((n,)),
            pltpu.SemaphoreType.DMA((n,)),
            pltpu.SemaphoreType.DMA,
            pltpu.SemaphoreType.REGULAR,
        ],
        compiler_params=pltpu.CompilerParams(collective_id=0, has_side_effects=True),
        name="exchange",
    )(send, meta, area)


def on_device(
    ny, nx,
    source_fields,
    diffusivity,
    cell_area,
    pair_block,
    pair_owner,
    pair_target,
    weight_blocks,
    target_area,
):
    n = ny * nx
    row_count = source_fields.shape[1]
    total_rows = row_count * ny
    row_start = lax.axis_index("ty") * row_count
    stacked = jnp.concatenate([source_fields, diffusivity[None]], axis=0)
    padded = padded_2(stacked, (("ty", 1), ("tx", 2)), 1)
    rate_padded = padded[-1]
    smoothed = diffuse(padded[:-1], rate_padded, row_start, total_rows)
    padded_again = padded_2(smoothed, (("ty", 1), ("tx", 2)), 1)
    smoothed = diffuse(padded_again, rate_padded, row_start, total_rows)
    scaled = (cell_area[None] * smoothed).astype(jnp.bfloat16)
    blocks = (
        scaled.reshape(NVAR, BR, BH, BCOL, BW)
        .transpose(1, 3, 0, 2, 4)
        .reshape(BR * BCOL, NVAR, BH * BW)
    )
    chosen = blocks[pair_block]
    partials = jnp.einsum("pvc,pcd->pvd", chosen, weight_blocks, preferred_element_type=jnp.float32)
    owners = pair_owner[:, 0]
    me = lax.axis_index("ty") * nx + lax.axis_index("tx")
    key = lax.rem(lax.rem(owners - me + n, n) * BACK, n)
    count = owners.shape[0]
    index = lax.iota(jnp.int32, count)
    same = (key[:, None] == key[None, :]) & (index[:, None] > index[None, :])
    rank = jnp.sum(same, axis=1)
    place = key * CAP + rank
    here = place[None, :] == lax.iota(jnp.int32, n * CAP)[:, None]
    source = jnp.sum(jnp.where(here, index[None, :], 0), axis=1)
    goal = jnp.sum(jnp.where(here, pair_target[None, :] + 1, 0), axis=1) - 1
    send = partials[source].reshape(n, CAP, NVAR, BH * BW)
    meta = jnp.pad(goal.reshape(n, 1, CAP), ((0, 0), (0, 0), (0, 128 - CAP)))
    return exchange(ny, nx, send, meta, target_area)


def solution(mesh):
    return jax.shard_map(
        functools.partial(on_device, mesh.shape["ty"], mesh.shape["tx"]),
        mesh=mesh,
        in_specs=(
            P(None, "ty", "tx"),
            P("ty", "tx"),
            P("ty", "tx"),
            P(("ty", "tx")),
            P(("ty", "tx"), None),
            P(("ty", "tx")),
            P(("ty", "tx"), None, None),
            P(("ty", "tx"), None),
        ),
        out_specs=P(("ty", "tx"), None, None),
        check_vma=False,
    )
```

```python
import functools

import jax
import jax.numpy as jnp
from jax import lax
from jax.experimental import pallas as pl
from jax.experimental.pallas import tpu as pltpu
from jax.sharding import PartitionSpec as P

NVAR = 8
BH = 8
BW = 16
BR = 12
BCOL = 16
TBD = 16
CAP = 4
CELLS = BH * BW
MESH = pl.DeviceIdType.MESH
STEP, BACK = 51, 123
GROUP = 16
SLOTS = GROUP // CAP


def kernel(
    ny, nx,
    fields_ref, rate_ref, area_ref, block_ref, owner_ref, target_ref, weight_ref, target_area_ref,
    out_ref,
    x, y, rate, k_east, k_west, k_north, k_south, pack, from_west, from_east, s0, s1,
    blocks, weights, part, send, got, tables, tables_smem, goal, meta, meta_got, meta_smem,
    local_sem, edge_send, edge_recv, data_send, data_recv, meta_send, meta_recv, ready,
):
    n = ny * nx
    rows, cols = rate_ref.shape
    pairs = weight_ref.shape[0]
    total_rows = rows * ny
    ty, tx = lax.axis_index("ty"), lax.axis_index("tx")
    me = ty * nx + tx
    north, south = lax.rem(ty + 1, ny), lax.rem(ty + ny - 1, ny)
    east, west = lax.rem(tx + 1, nx), lax.rem(tx + nx - 1, nx)
    corners = [(north, east), (north, west), (south, east), (south, west)]

    entry = pltpu.get_barrier_semaphore()
    mates = [(ty, lax.rem(tx + d, nx)) for d in range(1, nx)]
    mates += [(lax.rem(ty + d, ny), tx) for d in range(1, ny)]
    mates += corners
    for mate in mates:
        pl.semaphore_signal(entry, inc=1, device_id=mate, device_id_type=MESH)

    own = slice(8, 8 + rows)
    load_fields = pltpu.make_async_copy(fields_ref, x.at[:, own, 0:cols], local_sem.at[0])
    load_rate = pltpu.make_async_copy(rate_ref, rate.at[own, 0:cols], local_sem.at[1])
    load_weights = pltpu.make_async_copy(weight_ref, weights, local_sem.at[2])
    load_fields.start()
    load_rate.start()
    load_weights.start()
    load_fields.wait()
    load_rate.wait()

    lane = lax.broadcasted_iota(jnp.int32, (8, 128), 1)
    for i in range(rows // 8):
        band = slice(8 + 8 * i, 16 + 8 * i)
        packed = jnp.zeros((8, 128), jnp.float32)
        for v in range(NVAR + 1):
            if v < NVAR:
                first, last = x[v, band, 0:128], x[v, band, cols - 128:cols]
            else:
                first, last = rate[band, 0:128], rate[band, cols - 128:cols]
            edge = jnp.where(lane < 64, first, last)
            if v:
                edge = pltpu.roll(edge, 4 * v, 1)
            here = (lane >= 4 * v - 2) & (lane < 4 * v + 2)
            if v == 0:
                here = here | (lane >= 126)
            packed = jnp.where(here, edge, packed)
        pack[8 * i:8 * i + 8, :] = packed

    pl.semaphore_wait(entry, len(mates))

    def edge_copy(i, src, dst, device):
        return pltpu.make_async_remote_copy(
            src_ref=src, dst_ref=dst, send_sem=edge_send.at[i], recv_sem=edge_recv.at[i],
            device_id=device, device_id_type=MESH)

    low, high = slice(0, 8), slice(8 + rows, 16 + rows)
    top, bottom = slice(rows - 8, rows), slice(0, 8)
    edges = [
        (pack, from_west.at[own], (ty, east)),
        (pack, from_east.at[own], (ty, west)),
        (pack.at[top], from_west.at[low], corners[0]),
        (pack.at[top], from_east.at[low], corners[1]),
        (pack.at[bottom], from_west.at[high], corners[2]),
        (pack.at[bottom], from_east.at[high], corners[3]),
        (rate_ref.at[top], rate.at[low, 0:cols], (north, tx)),
        (rate_ref.at[bottom], rate.at[high, 0:cols], (south, tx)),
        (fields_ref.at[:, top], x.at[:, low, 0:cols], (north, tx)),
        (fields_ref.at[:, bottom], x.at[:, high, 0:cols], (south, tx)),
    ]
    edges = [edge_copy(i, *edge) for i, edge in enumerate(edges)]
    for edge in edges:
        edge.start()
    for d in range(1, ny):
        pl.semaphore_signal(ready, inc=1, device_id=(lax.rem(ty + d, ny), tx), device_id_type=MESH)

    p_lane = lax.broadcasted_iota(jnp.int32, (1, pairs), 1)
    p_row = lax.broadcasted_iota(jnp.int32, (pairs, 1), 0)
    key_row = jnp.bitwise_and((owner_ref[...] - me + n) * BACK, n - 1)
    joint_row = p_lane * 4096 + block_ref[...] * TBD + target_ref[...]
    goal_row = target_ref[...] + 1
    eye = lax.broadcasted_iota(jnp.int32, (pairs, pairs), 0) == lax.broadcasted_iota(jnp.int32, (pairs, pairs), 1)

    def along(axis, mask, value):
        return jnp.sum(jnp.where(mask, value, 0), axis=axis, keepdims=True, dtype=jnp.int32)

    unique_row = key_row * pairs + p_lane
    key_col = along(1, eye, key_row)
    joint_col = along(1, eye, joint_row)
    unique_col = key_col * pairs + p_row
    place_row = along(0, unique_col < unique_row, 1)
    place_col = along(1, unique_row < unique_col, 1)
    joint = along(0, place_col == p_lane, joint_col)
    tables[0:1, :] = jnp.clip(lax.shift_right_logical(joint, 12), 0, pairs - 1)
    tables[1:2, :] = jnp.clip(jnp.bitwise_and(lax.shift_right_logical(joint, 4), 255), 0, blocks.shape[0] - 1)
    tables[2:3, :] = along(0, key_col < p_lane, 1)
    table_copy = pltpu.make_async_copy(tables, tables_smem, local_sem.at[3])
    table_copy.start()

    d_col = lax.broadcasted_iota(jnp.int32, (n, 1), 0)
    rank = jnp.where(key_row == d_col, place_row - along(1, key_row < d_col, 1), -1)
    d_lane = lax.broadcasted_iota(jnp.int32, (n, 128), 1)
    goals = jnp.zeros((n, 128), jnp.int32)
    for k in range(CAP):
        goals = jnp.where(d_lane == k, along(1, rank == k, goal_row), goals)
    goal[...] = goals - 1
    for d in range(n):
        meta[d] = goal[d:d + 1, :]

    def peer(d):
        p = lax.rem(me + lax.rem(d * STEP, n), n)
        return (p // nx, lax.rem(p, nx))

    def meta_copy(d):
        return pltpu.make_async_remote_copy(
            src_ref=meta.at[d], dst_ref=meta_got.at[d], send_sem=meta_send.at[d],
            recv_sem=meta_recv.at[d], device_id=peer(d), device_id_type=MESH)

    def data_copy(d):
        return pltpu.make_async_remote_copy(
            src_ref=send.at[d], dst_ref=got.at[d], send_sem=data_send.at[d],
            recv_sem=data_recv.at[d], device_id=peer(d), device_id_type=MESH)

    def every(start, stop, action):
        def body(d, carry):
            action(d)
            return carry
        lax.fori_loop(start, stop, body, 0)

    pl.semaphore_wait(ready, ny - 1)
    meta_got[0] = meta[0]
    every(1, n, lambda d: meta_copy(d).start())

    for edge in edges:
        edge.wait()

    for i in range((rows + 16) // 8):
        band = slice(8 * i, 8 * i + 8)
        both = jnp.where(jnp.bitwise_and(lane, 3) < 2, from_east[band, :], from_west[band, :])
        for v in range(NVAR):
            x[v, band, cols:cols + 128] = pltpu.roll(both, (128 - 4 * v) % 128, 1) if v else both
        rate[band, cols:cols + 128] = pltpu.roll(both, 128 - 4 * NVAR, 1)

    wide = cols + 128
    bands = (rows + 8) // 8
    sub = lax.broadcasted_iota(jnp.int32, (8, wide), 0)
    for i in range(bands):
        a = 7 + 8 * i
        centre = rate[a:a + 8, :]
        g = sub + (ty * rows + 8 * i - 1)
        band = slice(8 * i, 8 * i + 8)
        k_east[band, :] = 0.5 * (centre + pltpu.roll(centre, wide - 1, 1))
        k_west[band, :] = 0.5 * (centre + pltpu.roll(centre, 1, 1))
        k_north[band, :] = jnp.where(g < total_rows - 1, 0.5 * (centre + rate[a + 1:a + 9, :]), 0.0)
        k_south[band, :] = jnp.where(g > 0, 0.5 * (centre + rate[a - 1:a + 7, :]), 0.0)

    def smooth(v, carry):
        for i in range(bands):
            a = 7 + 8 * i
            band = slice(8 * i, 8 * i + 8)
            c = x[v, a:a + 8, :]
            y[v, band, :] = (
                c
                + k_east[band, :] * (pltpu.roll(c, wide - 1, 1) - c)
                + k_west[band, :] * (pltpu.roll(c, 1, 1) - c)
                + k_north[band, :] * (x[v, a + 1:a + 9, :] - c)
                + k_south[band, :] * (x[v, a - 1:a + 7, :] - c)
            )
        for i in range(rows // 8):
            a = 8 * i + 1
            band = slice(a, a + 8)
            c = y[v, band, :]
            e = pltpu.roll(c, wide - 1, 1)[:, :cols]
            w = pltpu.roll(c, 1, 1)[:, :cols]
            c = c[:, :cols]
            z = (
                c
                + k_east[band, 0:cols] * (e - c)
                + k_west[band, 0:cols] * (w - c)
                + k_north[band, 0:cols] * (y[v, a + 1:a + 9, 0:cols] - c)
                + k_south[band, 0:cols] * (y[v, a - 1:a + 7, 0:cols] - c)
            )
            z = area_ref[8 * i:8 * i + 8, :] * z
            r = pl.multiple_of(v * rows + 8 * i, 8)
            s0[pl.ds(r, 8), :] = z[:, 0:128]
            s1[pl.ds(r, 8), :] = z[:, 128:256]
        return carry

    lax.fori_loop(0, NVAR, smooth, 0)

    def form(r, carry):
        for t, s in enumerate((s0, s1)):
            tiles = [s[pl.ds(r * BH + j, NVAR, stride=rows), :] for j in range(BH)]
            for bit in (1, 2, 4):
                mask = jnp.bitwise_and(lane, 16 * bit) == 0
                for j in range(BH):
                    if j & bit:
                        continue
                    lo, hi = tiles[j], tiles[j + bit]
                    tiles[j] = jnp.where(mask, lo, pltpu.roll(hi, 16 * bit, 1))
                    tiles[j + bit] = jnp.where(mask, pltpu.roll(lo, 128 - 16 * bit, 1), hi)
            for j in range(BH):
                blocks[r * BCOL + t * BH + j] = tiles[j]
        return carry

    lax.fori_loop(0, rows // BH, form, 0)

    table_copy.wait()
    load_weights.wait()

    def multiply(q):
        for u in range(GROUP):
            i = q * GROUP + u
            a = blocks[tables_smem[1, i]].astype(jnp.bfloat16)
            part[i] = jnp.dot(a, weights[tables_smem[0, i]], preferred_element_type=jnp.float32)

    def fill(q):
        for u in range(SLOTS):
            d = q * SLOTS + u
            first = tables_smem[2, d]
            for k in range(CAP):
                send[d, k] = part[jnp.minimum(first + k, pairs - 1)]

    def launch(q):
        for u in range(SLOTS):
            data_copy(q * SLOTS + u).start()

    last = n // SLOTS
    groups = pairs // GROUP
    multiply(0)
    fill(0)
    multiply(1)
    for u in range(1, SLOTS):
        data_copy(u).start()
    fill(1)
    multiply(2)

    def busy(q):
        launch(q - 2)
        fill(q - 1)
        multiply(q)

    def rest(q):
        launch(q - 2)
        fill(q - 1)

    every(3, groups, busy)
    every(groups, last + 1, rest)
    launch(last - 1)

    every(1, n, lambda d: meta_copy(d).wait())
    table = pltpu.make_async_copy(meta_got, meta_smem, local_sem.at[4])
    table.start()
    table.wait()

    def add(tiles, d, sums):
        sums = list(sums)
        for k in range(CAP):
            tile = tiles[d, k]
            t = meta_smem[d, 0, k]
            for j in range(TBD):
                sums[j] = sums[j] + jnp.where(t == j, tile, 0.0)
        return tuple(sums)

    def collect(d, sums):
        data_copy(d).wait()
        return add(got, d, sums)

    zero = jnp.zeros((NVAR, CELLS), jnp.float32)
    sums = add(send, 0, (zero,) * TBD)
    sums = lax.fori_loop(1, n, collect, sums)
    for j in range(TBD):
        out_ref[j] = sums[j] / target_area_ref[j:j + 1, :]


def on_device(
    ny, nx,
    source_fields,
    diffusivity,
    cell_area,
    pair_block,
    pair_owner,
    pair_target,
    weight_blocks,
    target_area,
):
    n = ny * nx
    nvar, rows, cols = source_fields.shape
    pairs = weight_blocks.shape[0]
    vmem = pl.BlockSpec(memory_space=pltpu.VMEM)
    hbm = pl.BlockSpec(memory_space=pltpu.HBM)
    f32, i32 = jnp.float32, jnp.int32
    wide, tall = cols + 128, rows + 16
    sem = pltpu.SemaphoreType.DMA
    return pl.pallas_call(
        functools.partial(kernel, ny, nx),
        out_shape=jax.ShapeDtypeStruct((TBD, NVAR, CELLS), f32),
        in_specs=[hbm, hbm, vmem, vmem, vmem, vmem, hbm, vmem],
        out_specs=vmem,
        scratch_shapes=[
            pltpu.VMEM((nvar, tall, wide), f32),
            pltpu.VMEM((nvar, tall, wide), f32),
            pltpu.VMEM((tall, wide), f32),
            pltpu.VMEM((tall, wide), f32),
            pltpu.VMEM((tall, wide), f32),
            pltpu.VMEM((tall, wide), f32),
            pltpu.VMEM((tall, wide), f32),
            pltpu.VMEM((rows, 128), f32),
            pltpu.VMEM((tall, 128), f32),
            pltpu.VMEM((tall, 128), f32),
            pltpu.VMEM((nvar * rows, 128), f32),
            pltpu.VMEM((nvar * rows, 128), f32),
            pltpu.VMEM((rows // BH * BCOL, NVAR, CELLS), f32),
            pltpu.VMEM((pairs, CELLS, CELLS), jnp.bfloat16),
            pltpu.VMEM((pairs, NVAR, CELLS), f32),
            pltpu.VMEM((n, CAP, NVAR, CELLS), f32),
            pltpu.VMEM((n, CAP, NVAR, CELLS), f32),
            pltpu.VMEM((8, pairs), i32),
            pltpu.SMEM((8, pairs), i32),
            pltpu.VMEM((n, 128), i32),
            pltpu.VMEM((n, 1, 128), i32),
            pltpu.VMEM((n, 1, 128), i32),
            pltpu.SMEM((n, 1, 128), i32),
            sem((5,)),
            sem((10,)),
            sem((10,)),
            sem((n,)),
            sem((n,)),
            sem((n,)),
            sem((n,)),
            pltpu.SemaphoreType.REGULAR,
        ],
        compiler_params=pltpu.CompilerParams(
            collective_id=0, has_side_effects=True, vmem_limit_bytes=62 * 1024 * 1024),
        name="regrid",
    )(
        source_fields, diffusivity, cell_area, pair_block.reshape(1, pairs), pair_owner.reshape(1, pairs),
        pair_target.reshape(1, pairs), weight_blocks, target_area,
    )


def solution(mesh):
    return jax.shard_map(
        functools.partial(on_device, mesh.shape["ty"], mesh.shape["tx"]),
        mesh=mesh,
        in_specs=(
            P(None, "ty", "tx"),
            P("ty", "tx"),
            P("ty", "tx"),
            P(("ty", "tx")),
            P(("ty", "tx"), None),
            P(("ty", "tx")),
            P(("ty", "tx"), None, None),
            P(("ty", "tx"), None),
        ),
        out_specs=P(("ty", "tx"), None, None),
        check_vma=False,
    )
```

```python
import functools

import jax
import jax.numpy as jnp
from jax import lax
from jax.experimental import pallas as pl
from jax.experimental.pallas import tpu as pltpu
from jax.sharding import PartitionSpec as P

NVAR = 8
BH = 8
BW = 16
BR = 12
BCOL = 16
TBD = 16
CAP = 4
CELLS = BH * BW
MESH = pl.DeviceIdType.MESH
STEP, BACK = 51, 123
GROUP = 16
SLOTS = GROUP // CAP
FOLD = 4
FORM = 3


def kernel(
    ny, nx,
    fields_ref, rate_ref, area_ref, block_ref, owner_ref, target_ref, weight_ref, target_area_ref,
    out_ref,
    x, y, rate, k_east, k_west, k_north, k_south, pack, from_west, from_east,
    up, down, from_south, from_north, s0, s1,
    blocks, weights, part, send, got, tables, tables_smem, goal, relay, sorted_goal, goal_got, goal_smem,
    local_sem, edge_send, edge_recv, data_send, data_recv, goal_send, goal_recv, ready,
):
    n = ny * nx
    rows, cols = rate_ref.shape
    pairs = weight_ref.shape[0]
    total_rows = rows * ny
    ty, tx = lax.axis_index("ty"), lax.axis_index("tx")
    me = ty * nx + tx
    north, south = lax.rem(ty + 1, ny), lax.rem(ty + ny - 1, ny)
    east, west = lax.rem(tx + 1, nx), lax.rem(tx + nx - 1, nx)
    corners = [(north, east), (north, west), (south, east), (south, west)]

    entry = pltpu.get_barrier_semaphore()
    mates = [(ty, lax.rem(tx + d, nx)) for d in range(1, nx)]
    mates += [(lax.rem(ty + d, ny), tx) for d in range(1, ny)]
    mates += corners
    for mate in mates:
        pl.semaphore_signal(entry, inc=1, device_id=mate, device_id_type=MESH)

    own = slice(8, 8 + rows)
    load_fields = pltpu.make_async_copy(fields_ref, x.at[:, own, 0:cols], local_sem.at[0])
    load_rate = pltpu.make_async_copy(rate_ref, rate.at[own, 0:cols], local_sem.at[1])
    load_weights = pltpu.make_async_copy(weight_ref, weights, local_sem.at[2])
    load_fields.start()
    load_rate.start()
    load_weights.start()
    load_fields.wait()
    load_rate.wait()

    lane = lax.broadcasted_iota(jnp.int32, (8, 128), 1)
    for j in range(FOLD):
        packed = jnp.zeros((8, 128), jnp.float32)
        for g in range(rows // (8 * FOLD)):
            a = 8 + 8 * (j + FOLD * g)
            for v in range(NVAR + 1):
                field = x.at[v] if v < NVAR else rate
                edge = jnp.where(lane < 64, field[a:a + 8, 0:128], field[a:a + 8, cols - 128:cols])
                at = 40 * g + 4 * v
                edge = pltpu.roll(edge, at + 2, 1)
                packed = jnp.where((lane >= at) & (lane < at + 4), edge, packed)
        pack[8 * j:8 * j + 8, :] = packed
    for v in range(NVAR + 1):
        field = x.at[v] if v < NVAR else rate
        up[2 * v:2 * v + 2, :] = field[6 + rows:8 + rows, 0:cols]
        down[2 * v:2 * v + 2, :] = field[8:10, 0:cols]

    pl.semaphore_wait(entry, len(mates))

    def edge_copy(i, src, dst, device):
        return pltpu.make_async_remote_copy(
            src_ref=src, dst_ref=dst, send_sem=edge_send.at[i], recv_sem=edge_recv.at[i],
            device_id=device, device_id_type=MESH)

    main, low, high = slice(8, 8 + 8 * FOLD), slice(0, 8), slice(8 + 8 * FOLD, 16 + 8 * FOLD)
    top, bottom = slice(8 * FOLD - 8, 8 * FOLD), slice(0, 8)
    edges = [
        (pack.at[top], from_west.at[low], corners[0]),
        (pack.at[top], from_east.at[low], corners[1]),
        (pack.at[bottom], from_west.at[high], corners[2]),
        (pack.at[bottom], from_east.at[high], corners[3]),
        (pack, from_west.at[main], (ty, east)),
        (pack, from_east.at[main], (ty, west)),
        (up, from_south, (north, tx)),
        (down, from_north, (south, tx)),
    ]
    edges = [edge_copy(i, *edge) for i, edge in enumerate(edges)]
    for edge in edges:
        edge.start()
    for d in range(1, ny):
        pl.semaphore_signal(ready, inc=1, device_id=(lax.rem(ty + d, ny), tx), device_id_type=MESH)

    p_lane = lax.broadcasted_iota(jnp.int32, (1, pairs), 1)
    p_row = lax.broadcasted_iota(jnp.int32, (pairs, 1), 0)
    key_row = jnp.bitwise_and((owner_ref[...] - me + n) * BACK, n - 1)
    joint_row = p_lane * 4096 + block_ref[...] * TBD + target_ref[...]
    goal_row = target_ref[...] + 1
    eye = lax.broadcasted_iota(jnp.int32, (pairs, pairs), 0) == lax.broadcasted_iota(jnp.int32, (pairs, pairs), 1)

    def along(axis, mask, value):
        return jnp.sum(jnp.where(mask, value, 0), axis=axis, keepdims=True, dtype=jnp.int32)

    unique_row = key_row * pairs + p_lane
    key_col = along(1, eye, key_row)
    joint_col = along(1, eye, joint_row)
    unique_col = key_col * pairs + p_row
    place_row = along(0, unique_col < unique_row, 1)
    place_col = along(1, unique_row < unique_col, 1)
    joint = along(0, place_col == p_lane, joint_col)
    tables[0:1, :] = jnp.clip(lax.shift_right_logical(joint, 12), 0, pairs - 1)
    tables[1:2, :] = jnp.clip(jnp.bitwise_and(lax.shift_right_logical(joint, 4), 255), 0, blocks.shape[0] - 1)
    tables[2:3, :] = along(0, key_col < p_lane, 1)
    table_copy = pltpu.make_async_copy(tables, tables_smem, local_sem.at[3])
    table_copy.start()

    r_col = lax.broadcasted_iota(jnp.int32, (n, 1), 0)
    owner_col = lax.rem(r_col, ny) * nx + lax.div(r_col, ny)
    d_col = jnp.bitwise_and((owner_col - me + n) * BACK, n - 1)
    rank = jnp.where(key_row == d_col, place_row - along(1, key_row < d_col, 1), -1)
    d_lane = lax.broadcasted_iota(jnp.int32, (n, 128), 1)
    goals = jnp.zeros((n, 128), jnp.int32)
    for k in range(CAP):
        goals = jnp.where(d_lane == k, along(1, rank == k, goal_row), goals)
    goal[...] = goals - 1

    def rows_of(i, size):
        return pl.ds(pl.multiple_of(i * size, 8), size)

    def goal_copy(i, src, dst, device):
        return pltpu.make_async_remote_copy(
            src_ref=src, dst_ref=dst, send_sem=goal_send.at[i], recv_sem=goal_recv.at[i],
            device_id=device, device_id_type=MESH)

    along_tx, along_ty = [], []
    for d in range(1, nx):
        to = lax.rem(tx + d, nx)
        along_tx.append(goal_copy(d, goal.at[rows_of(to, ny)], relay.at[rows_of(tx, ny)], (ty, to)))
    for d in range(1, ny):
        to = lax.rem(ty + d, ny)
        along_ty.append(goal_copy(nx + d, sorted_goal.at[rows_of(to, nx)], goal_got.at[rows_of(ty, nx)], (to, tx)))
    for copy in along_tx:
        copy.start()
    relay[rows_of(tx, ny), :] = goal[rows_of(tx, ny), :]

    def peer(d):
        p = lax.rem(me + lax.rem(d * STEP, n), n)
        return (p // nx, lax.rem(p, nx))

    def data_copy(d):
        return pltpu.make_async_remote_copy(
            src_ref=send.at[d], dst_ref=got.at[d], send_sem=data_send.at[d],
            recv_sem=data_recv.at[d], device_id=peer(d), device_id_type=MESH)

    def every(start, stop, action):
        def body(d, carry):
            action(d)
            return carry
        lax.fori_loop(start, stop, body, 0)

    for edge in edges:
        edge.wait()

    both = []
    for i in range(FOLD + 2):
        band = slice(8 * i, 8 * i + 8)
        both.append(jnp.where(jnp.bitwise_and(lane, 3) < 2, from_west[band, :], from_east[band, :]))
    folds = rows // (8 * FOLD)
    for i in range(-1, rows // 8 + 1):
        if i < 0:
            tile, g = both[0], folds - 1
        elif i == rows // 8:
            tile, g = both[-1], 0
        else:
            tile, g = both[1 + i % FOLD], i // FOLD
        band = slice(8 + 8 * i, 16 + 8 * i)
        for v in range(NVAR + 1):
            field = x.at[v] if v < NVAR else rate
            field[band, cols:cols + 128] = pltpu.roll(tile, 126 - 40 * g - 4 * v, 1)
    for v in range(NVAR + 1):
        field = x.at[v] if v < NVAR else rate
        field[6:8, 0:cols] = from_south[2 * v:2 * v + 2, :]
        field[8 + rows:10 + rows, 0:cols] = from_north[2 * v:2 * v + 2, :]

    wide = cols + 128
    bands = (rows + 8) // 8
    sub = lax.broadcasted_iota(jnp.int32, (8, wide), 0)
    for i in range(bands):
        a = 7 + 8 * i
        centre = rate[a:a + 8, :]
        g = sub + (ty * rows + 8 * i - 1)
        band = slice(8 * i, 8 * i + 8)
        k_east[band, :] = 0.5 * (centre + pltpu.roll(centre, wide - 1, 1))
        k_west[band, :] = 0.5 * (centre + pltpu.roll(centre, 1, 1))
        k_north[band, :] = jnp.where(g < total_rows - 1, 0.5 * (centre + rate[a + 1:a + 9, :]), 0.0)
        k_south[band, :] = jnp.where(g > 0, 0.5 * (centre + rate[a - 1:a + 7, :]), 0.0)

    def smooth(v, carry):
        for i in range(bands):
            a = 7 + 8 * i
            band = slice(8 * i, 8 * i + 8)
            c = x[v, a:a + 8, :]
            y[v, band, :] = (
                c
                + k_east[band, :] * (pltpu.roll(c, wide - 1, 1) - c)
                + k_west[band, :] * (pltpu.roll(c, 1, 1) - c)
                + k_north[band, :] * (x[v, a + 1:a + 9, :] - c)
                + k_south[band, :] * (x[v, a - 1:a + 7, :] - c)
            )
        for i in range(rows // 8):
            a = 8 * i + 1
            band = slice(a, a + 8)
            c = y[v, band, :]
            e = pltpu.roll(c, wide - 1, 1)[:, :cols]
            w = pltpu.roll(c, 1, 1)[:, :cols]
            c = c[:, :cols]
            z = (
                c
                + k_east[band, 0:cols] * (e - c)
                + k_west[band, 0:cols] * (w - c)
                + k_north[band, 0:cols] * (y[v, a + 1:a + 9, 0:cols] - c)
                + k_south[band, 0:cols] * (y[v, a - 1:a + 7, 0:cols] - c)
            )
            z = area_ref[8 * i:8 * i + 8, :] * z
            r = pl.multiple_of(v * rows + 8 * i, 8)
            s0[pl.ds(r, 8), :] = z[:, 0:128]
            s1[pl.ds(r, 8), :] = z[:, 128:256]
        return carry

    lax.fori_loop(0, NVAR, smooth, 0)

    def form(q, carry):
        group = [(q * FORM + u, t, s) for u in range(FORM) for t, s in enumerate((s0, s1))]
        tiles = [[s[pl.ds(r * BH + j, NVAR, stride=rows), :] for j in range(BH)] for r, t, s in group]
        for bit in (1, 2, 4):
            mask = jnp.bitwise_and(lane, 16 * bit) == 0
            for tile in tiles:
                for j in range(BH):
                    if j & bit:
                        continue
                    lo, hi = tile[j], tile[j + bit]
                    tile[j] = jnp.where(mask, lo, pltpu.roll(hi, 16 * bit, 1))
                    tile[j + bit] = jnp.where(mask, pltpu.roll(lo, 128 - 16 * bit, 1), hi)
        for (r, t, s), tile in zip(group, tiles):
            for j in range(BH):
                blocks[r * BCOL + t * BH + j] = tile[j]
        return carry

    lax.fori_loop(0, rows // BH // FORM, form, 0)

    table_copy.wait()
    load_weights.wait()

    def multiply(q):
        for u in range(GROUP):
            i = q * GROUP + u
            a = blocks[tables_smem[1, i]].astype(jnp.bfloat16)
            part[i] = jnp.dot(a, weights[tables_smem[0, i]], preferred_element_type=jnp.float32)

    def fill(q):
        for u in range(SLOTS):
            d = q * SLOTS + u
            first = tables_smem[2, d]
            for k in range(CAP):
                send[d, k] = part[jnp.minimum(first + k, pairs - 1)]

    def launch(q):
        for u in range(SLOTS):
            data_copy(q * SLOTS + u).start()

    last = n // SLOTS
    groups = pairs // GROUP
    multiply(0)
    fill(0)
    multiply(1)
    pl.semaphore_wait(ready, ny - 1)
    for u in range(1, SLOTS):
        data_copy(u).start()
    fill(1)
    multiply(2)

    for copy in along_tx:
        copy.wait()
    for i in range(ny):
        sorted_goal[i * nx:(i + 1) * nx, :] = relay[pl.ds(i, nx, stride=ny), :]
    goal_got[rows_of(ty, nx), :] = sorted_goal[rows_of(ty, nx), :]
    launch(1)
    fill(2)
    multiply(3)
    for copy in along_ty:
        copy.start()

    def busy(q):
        launch(q - 2)
        fill(q - 1)
        multiply(q)

    def rest(q):
        launch(q - 2)
        fill(q - 1)

    every(4, groups, busy)
    every(groups, last + 1, rest)
    launch(last - 1)

    for copy in along_ty:
        copy.wait()
    goal_table = pltpu.make_async_copy(goal_got, goal_smem, local_sem.at[4])
    goal_table.start()
    goal_table.wait()

    def add(tiles, d, sums):
        sums = list(sums)
        source = lax.rem(me + (n - d) * STEP, n)
        for k in range(CAP):
            tile = tiles[d, k]
            t = goal_smem[source, k]
            for j in range(TBD):
                sums[j] = sums[j] + jnp.where(t == j, tile, 0.0)
        return tuple(sums)

    def collect(d, sums):
        data_copy(d).wait()
        return add(got, d, sums)

    zero = jnp.zeros((NVAR, CELLS), jnp.float32)
    sums = add(send, 0, (zero,) * TBD)
    sums = lax.fori_loop(1, n, collect, sums)
    for j in range(TBD):
        out_ref[j] = sums[j] / target_area_ref[j:j + 1, :]


def on_device(
    ny, nx,
    source_fields,
    diffusivity,
    cell_area,
    pair_block,
    pair_owner,
    pair_target,
    weight_blocks,
    target_area,
):
    n = ny * nx
    nvar, rows, cols = source_fields.shape
    pairs = weight_blocks.shape[0]
    vmem = pl.BlockSpec(memory_space=pltpu.VMEM)
    hbm = pl.BlockSpec(memory_space=pltpu.HBM)
    f32, i32 = jnp.float32, jnp.int32
    wide, tall = cols + 128, rows + 16
    sem = pltpu.SemaphoreType.DMA
    return pl.pallas_call(
        functools.partial(kernel, ny, nx),
        out_shape=jax.ShapeDtypeStruct((TBD, NVAR, CELLS), f32),
        in_specs=[hbm, hbm, vmem, vmem, vmem, vmem, hbm, vmem],
        out_specs=vmem,
        scratch_shapes=[
            pltpu.VMEM((nvar, tall, wide), f32),
            pltpu.VMEM((nvar, tall, wide), f32),
            pltpu.VMEM((tall, wide), f32),
            pltpu.VMEM((tall, wide), f32),
            pltpu.VMEM((tall, wide), f32),
            pltpu.VMEM((tall, wide), f32),
            pltpu.VMEM((tall, wide), f32),
            pltpu.VMEM((8 * FOLD, 128), f32),
            pltpu.VMEM((8 * FOLD + 16, 128), f32),
            pltpu.VMEM((8 * FOLD + 16, 128), f32),
            pltpu.VMEM((24, cols), f32),
            pltpu.VMEM((24, cols), f32),
            pltpu.VMEM((24, cols), f32),
            pltpu.VMEM((24, cols), f32),
            pltpu.VMEM((nvar * rows, 128), f32),
            pltpu.VMEM((nvar * rows, 128), f32),
            pltpu.VMEM((rows // BH * BCOL, NVAR, CELLS), f32),
            pltpu.VMEM((pairs, CELLS, CELLS), jnp.bfloat16),
            pltpu.VMEM((pairs, NVAR, CELLS), f32),
            pltpu.VMEM((n, CAP, NVAR, CELLS), f32),
            pltpu.VMEM((n, CAP, NVAR, CELLS), f32),
            pltpu.VMEM((8, pairs), i32),
            pltpu.SMEM((8, pairs), i32),
            pltpu.VMEM((n, 128), i32),
            pltpu.VMEM((n, 128), i32),
            pltpu.VMEM((n, 128), i32),
            pltpu.VMEM((n, 128), i32),
            pltpu.SMEM((n, 128), i32),
            sem((5,)),
            sem((8,)),
            sem((8,)),
            sem((n,)),
            sem((n,)),
            sem((nx + ny,)),
            sem((nx + ny,)),
            pltpu.SemaphoreType.REGULAR,
        ],
        compiler_params=pltpu.CompilerParams(
            collective_id=0, has_side_effects=True, vmem_limit_bytes=62 * 1024 * 1024),
        name="regrid",
    )(
        source_fields, diffusivity, cell_area, pair_block.reshape(1, pairs), pair_owner.reshape(1, pairs),
        pair_target.reshape(1, pairs), weight_blocks, target_area,
    )


def solution(mesh):
    return jax.shard_map(
        functools.partial(on_device, mesh.shape["ty"], mesh.shape["tx"]),
        mesh=mesh,
        in_specs=(
            P(None, "ty", "tx"),
            P("ty", "tx"),
            P("ty", "tx"),
            P(("ty", "tx")),
            P(("ty", "tx"), None),
            P(("ty", "tx")),
            P(("ty", "tx"), None, None),
            P(("ty", "tx"), None),
        ),
        out_specs=P(("ty", "tx"), None, None),
        check_vma=False,
    )
```

```python
import functools

import jax
import jax.numpy as jnp
from jax import lax
from jax.experimental import pallas as pl
from jax.experimental.pallas import tpu as pltpu
from jax.sharding import PartitionSpec as P

NVAR = 8
BH = 8
BW = 16
BR = 12
BCOL = 16
TBD = 16
CAP = 4
CELLS = BH * BW
MESH = pl.DeviceIdType.MESH
STEP, BACK = 51, 123
GROUP = 16
SLOTS = GROUP // CAP
FOLD = 4
BATCH = 8
FORM = 3


def kernel(
    ny, nx,
    fields_hbm, rate_hbm, area_hbm, block_hbm, owner_hbm, target_hbm, weight_hbm, target_area_hbm,
    out_ref,
    area_ref, block_ref, owner_ref, target_ref, target_area_ref,
    x, y, rate, k_east, k_west, k_north, k_south, pack, from_west, from_east,
    up, down, from_south, from_north, s0, s1,
    blocks, weights, part, send, got, tables, tables_smem, goal, relay, sorted_goal, goal_got, goal_smem,
    local_sem, edge_send, edge_recv, data_send, data_recv, goal_send, goal_recv, ready,
):
    n = ny * nx
    rows, cols = rate_hbm.shape
    pairs = weight_hbm.shape[0]
    total_rows = rows * ny
    ty, tx = lax.axis_index("ty"), lax.axis_index("tx")
    me = ty * nx + tx
    north, south = lax.rem(ty + 1, ny), lax.rem(ty + ny - 1, ny)
    east, west = lax.rem(tx + 1, nx), lax.rem(tx + nx - 1, nx)
    corners = [(north, east), (north, west), (south, east), (south, west)]

    entry = pltpu.get_barrier_semaphore()
    mates = [(ty, lax.rem(tx + d, nx)) for d in range(1, nx)]
    mates += [(lax.rem(ty + d, ny), tx) for d in range(1, ny)]
    mates += corners
    for mate in mates:
        pl.semaphore_signal(entry, inc=1, device_id=mate, device_id_type=MESH)

    own = slice(8, 8 + rows)
    loads = [
        (fields_hbm, x.at[:, own, 0:cols]),
        (rate_hbm, rate.at[own, 0:cols]),
        (block_hbm, block_ref),
        (owner_hbm, owner_ref),
        (target_hbm, target_ref),
        (area_hbm, area_ref),
        (target_area_hbm, target_area_ref),
        (weight_hbm, weights),
    ]
    loads = [pltpu.make_async_copy(src, dst, local_sem.at[i]) for i, (src, dst) in enumerate(loads)]
    for load in loads:
        load.start()
    for load in loads[:2]:
        load.wait()

    lane = lax.broadcasted_iota(jnp.int32, (8, 128), 1)
    for j in range(FOLD):
        packed = jnp.zeros((8, 128), jnp.float32)
        for g in range(rows // (8 * FOLD)):
            a = 8 + 8 * (j + FOLD * g)
            for v in range(NVAR + 1):
                field = x.at[v] if v < NVAR else rate
                edge = jnp.where(lane < 64, field[a:a + 8, 0:128], field[a:a + 8, cols - 128:cols])
                at = 40 * g + 4 * v
                edge = pltpu.roll(edge, at + 2, 1)
                packed = jnp.where((lane >= at) & (lane < at + 4), edge, packed)
        pack[8 * j:8 * j + 8, :] = packed
    for v in range(NVAR + 1):
        field = x.at[v] if v < NVAR else rate
        up[2 * v:2 * v + 2, :] = field[6 + rows:8 + rows, 0:cols]
        down[2 * v:2 * v + 2, :] = field[8:10, 0:cols]

    pl.semaphore_wait(entry, len(mates))

    def edge_copy(i, src, dst, device):
        return pltpu.make_async_remote_copy(
            src_ref=src, dst_ref=dst, send_sem=edge_send.at[i], recv_sem=edge_recv.at[i],
            device_id=device, device_id_type=MESH)

    main, low, high = slice(8, 8 + 8 * FOLD), slice(0, 8), slice(8 + 8 * FOLD, 16 + 8 * FOLD)
    top, bottom = slice(8 * FOLD - 8, 8 * FOLD), slice(0, 8)
    edges = [
        (0, pack.at[top], from_west.at[low], corners[0]),
        (1, pack.at[top], from_east.at[low], corners[1]),
        (0, pack.at[bottom], from_west.at[high], corners[2]),
        (1, pack.at[bottom], from_east.at[high], corners[3]),
        (0, pack, from_west.at[main], (ty, east)),
        (1, pack, from_east.at[main], (ty, west)),
        (2, up, from_south, (north, tx)),
        (3, down, from_north, (south, tx)),
    ]
    for edge in edges:
        edge_copy(*edge).start()
    for d in range(1, ny):
        pl.semaphore_signal(ready, inc=1, device_id=(lax.rem(ty + d, ny), tx), device_id_type=MESH)

    for load in loads[2:5]:
        load.wait()
    p_lane = lax.broadcasted_iota(jnp.int32, (1, pairs), 1)
    p_row = lax.broadcasted_iota(jnp.int32, (pairs, 1), 0)
    key_row = jnp.bitwise_and((owner_ref[...] - me + n) * BACK, n - 1)
    joint_row = p_lane * 4096 + block_ref[...] * TBD + target_ref[...]
    goal_row = target_ref[...] + 1
    eye = lax.broadcasted_iota(jnp.int32, (pairs, pairs), 0) == lax.broadcasted_iota(jnp.int32, (pairs, pairs), 1)

    def along(axis, mask, value):
        return jnp.sum(jnp.where(mask, value, 0), axis=axis, keepdims=True, dtype=jnp.int32)

    unique_row = key_row * pairs + p_lane
    key_col = along(1, eye, key_row)
    joint_col = along(1, eye, joint_row)
    unique_col = key_col * pairs + p_row
    place_row = along(0, unique_col < unique_row, 1)
    place_col = along(1, unique_row < unique_col, 1)
    joint = along(0, place_col == p_lane, joint_col)
    tables[0:1, :] = jnp.clip(lax.shift_right_logical(joint, 12), 0, pairs - 1)
    tables[1:2, :] = jnp.clip(jnp.bitwise_and(lax.shift_right_logical(joint, 4), 255), 0, blocks.shape[0] - 1)
    tables[2:3, :] = along(0, key_col < p_lane, 1)
    table_copy = pltpu.make_async_copy(tables, tables_smem, local_sem.at[8])
    table_copy.start()

    r_col = lax.broadcasted_iota(jnp.int32, (n, 1), 0)
    owner_col = lax.rem(r_col, ny) * nx + lax.div(r_col, ny)
    d_col = jnp.bitwise_and((owner_col - me + n) * BACK, n - 1)
    rank = jnp.where(key_row == d_col, place_row - along(1, key_row < d_col, 1), -1)
    d_lane = lax.broadcasted_iota(jnp.int32, (n, 128), 1)
    goals = jnp.zeros((n, 128), jnp.int32)
    for k in range(CAP):
        goals = jnp.where(d_lane == k, along(1, rank == k, goal_row), goals)
    goal[...] = goals - 1

    def rows_of(i, size):
        return pl.ds(pl.multiple_of(i * size, 8), size)

    def goal_copy(i, src, dst, device):
        return pltpu.make_async_remote_copy(
            src_ref=src, dst_ref=dst, send_sem=goal_send.at[i], recv_sem=goal_recv.at[i],
            device_id=device, device_id_type=MESH)

    along_tx, along_ty = [], []
    for d in range(1, nx):
        to = lax.rem(tx + d, nx)
        along_tx.append(goal_copy(0, goal.at[rows_of(to, ny)], relay.at[d * ny:(d + 1) * ny], (ty, to)))
    for d in range(1, ny):
        to = lax.rem(ty + d, ny)
        along_ty.append(goal_copy(1, sorted_goal.at[rows_of(to, nx)], goal_got.at[d * nx:(d + 1) * nx], (to, tx)))
    for copy in along_tx:
        copy.start()
    relay[0:ny, :] = goal[rows_of(tx, ny), :]

    def peer(d):
        p = lax.rem(me + lax.rem(d * STEP, n), n)
        return (p // nx, lax.rem(p, nx))

    def data_copy(d):
        return pltpu.make_async_remote_copy(
            src_ref=send.at[d], dst_ref=got.at[d], send_sem=data_send,
            recv_sem=data_recv.at[lax.div(d, BATCH)], device_id=peer(d), device_id_type=MESH)

    def every(start, stop, action):
        def body(d, carry):
            action(d)
            return carry
        lax.fori_loop(start, stop, body, 0)

    for i, landed in enumerate((from_west, from_east, from_south, from_north)):
        edge_copy(i, landed, landed, (ty, east)).wait()

    both = []
    for i in range(FOLD + 2):
        band = slice(8 * i, 8 * i + 8)
        both.append(jnp.where(jnp.bitwise_and(lane, 3) < 2, from_west[band, :], from_east[band, :]))
    folds = rows // (8 * FOLD)
    for i in range(-1, rows // 8 + 1):
        if i < 0:
            tile, g = both[0], folds - 1
        elif i == rows // 8:
            tile, g = both[-1], 0
        else:
            tile, g = both[1 + i % FOLD], i // FOLD
        band = slice(8 + 8 * i, 16 + 8 * i)
        for v in range(NVAR + 1):
            field = x.at[v] if v < NVAR else rate
            field[band, cols:cols + 128] = pltpu.roll(tile, 126 - 40 * g - 4 * v, 1)
    for v in range(NVAR + 1):
        field = x.at[v] if v < NVAR else rate
        field[6:8, 0:cols] = from_south[2 * v:2 * v + 2, :]
        field[8 + rows:10 + rows, 0:cols] = from_north[2 * v:2 * v + 2, :]

    wide = cols + 128
    bands = (rows + 8) // 8
    sub = lax.broadcasted_iota(jnp.int32, (8, wide), 0)
    for i in range(bands):
        a = 7 + 8 * i
        centre = rate[a:a + 8, :]
        g = sub + (ty * rows + 8 * i - 1)
        band = slice(8 * i, 8 * i + 8)
        k_east[band, :] = 0.5 * (centre + pltpu.roll(centre, wide - 1, 1))
        k_west[band, :] = 0.5 * (centre + pltpu.roll(centre, 1, 1))
        k_north[band, :] = jnp.where(g < total_rows - 1, 0.5 * (centre + rate[a + 1:a + 9, :]), 0.0)
        k_south[band, :] = jnp.where(g > 0, 0.5 * (centre + rate[a - 1:a + 7, :]), 0.0)

    def smooth(v, carry):
        for i in range(bands):
            a = 7 + 8 * i
            band = slice(8 * i, 8 * i + 8)
            c = x[v, a:a + 8, :]
            y[v, band, :] = (
                c
                + k_east[band, :] * (pltpu.roll(c, wide - 1, 1) - c)
                + k_west[band, :] * (pltpu.roll(c, 1, 1) - c)
                + k_north[band, :] * (x[v, a + 1:a + 9, :] - c)
                + k_south[band, :] * (x[v, a - 1:a + 7, :] - c)
            )
        for i in range(rows // 8):
            a = 8 * i + 1
            band = slice(a, a + 8)
            c = y[v, band, :]
            e = pltpu.roll(c, wide - 1, 1)[:, :cols]
            w = pltpu.roll(c, 1, 1)[:, :cols]
            c = c[:, :cols]
            z = (
                c
                + k_east[band, 0:cols] * (e - c)
                + k_west[band, 0:cols] * (w - c)
                + k_north[band, 0:cols] * (y[v, a + 1:a + 9, 0:cols] - c)
                + k_south[band, 0:cols] * (y[v, a - 1:a + 7, 0:cols] - c)
            )
            z = area_ref[8 * i:8 * i + 8, :] * z
            r = pl.multiple_of(v * rows + 8 * i, 8)
            s0[pl.ds(r, 8), :] = z[:, 0:128]
            s1[pl.ds(r, 8), :] = z[:, 128:256]
        return carry

    loads[5].wait()
    lax.fori_loop(0, NVAR, smooth, 0)

    def form(q, carry):
        group = [(q * FORM + u, t, s) for u in range(FORM) for t, s in enumerate((s0, s1))]
        tiles = [[s[pl.ds(r * BH + j, NVAR, stride=rows), :] for j in range(BH)] for r, t, s in group]
        for bit in (1, 2, 4):
            mask = jnp.bitwise_and(lane, 16 * bit) == 0
            for tile in tiles:
                for j in range(BH):
                    if j & bit:
                        continue
                    lo, hi = tile[j], tile[j + bit]
                    tile[j] = jnp.where(mask, lo, pltpu.roll(hi, 16 * bit, 1))
                    tile[j + bit] = jnp.where(mask, pltpu.roll(lo, 128 - 16 * bit, 1), hi)
        for (r, t, s), tile in zip(group, tiles):
            for j in range(BH):
                blocks[r * BCOL + t * BH + j] = tile[j]
        return carry

    lax.fori_loop(0, rows // BH // FORM, form, 0)

    table_copy.wait()
    for load in loads[6:]:
        load.wait()

    def multiply(q):
        for u in range(GROUP):
            i = q * GROUP + u
            a = blocks[tables_smem[1, i]].astype(jnp.bfloat16)
            part[i] = jnp.dot(a, weights[tables_smem[0, i]], preferred_element_type=jnp.float32)

    def fill(q):
        for u in range(SLOTS):
            d = q * SLOTS + u
            first = tables_smem[2, d]
            for k in range(CAP):
                send[d, k] = part[jnp.minimum(first + k, pairs - 1)]

    def launch(q):
        for u in range(SLOTS):
            data_copy(q * SLOTS + u).start()

    last = n // SLOTS
    groups = pairs // GROUP
    multiply(0)
    fill(0)
    multiply(1)
    pl.semaphore_wait(ready, ny - 1)
    for u in range(1, SLOTS):
        data_copy(u).start()
    fill(1)
    multiply(2)

    landed = relay.at[ny:n]
    goal_copy(0, landed, landed, (ty, east)).wait()
    for i in range(ny):
        sorted_goal[i * nx:(i + 1) * nx, :] = relay[pl.ds(i, nx, stride=ny), :]
    goal_got[0:nx, :] = sorted_goal[rows_of(ty, nx), :]
    launch(1)
    fill(2)
    multiply(3)
    for copy in along_ty:
        copy.start()

    def busy(q):
        launch(q - 2)
        fill(q - 1)
        multiply(q)

    def rest(q):
        launch(q - 2)
        fill(q - 1)

    every(4, groups, busy)
    every(groups, last + 1, rest)
    launch(last - 1)

    landed = goal_got.at[nx:n]
    goal_copy(1, landed, landed, (north, tx)).wait()
    goal_table = pltpu.make_async_copy(goal_got, goal_smem, local_sem.at[9])
    goal_table.start()
    goal_table.wait()

    def arrived(b, start, size):
        landed = got.at[pl.ds(start, size)]
        return pltpu.make_async_remote_copy(
            src_ref=landed, dst_ref=landed, send_sem=data_send, recv_sem=data_recv.at[b],
            device_id=(ty, east), device_id_type=MESH)

    def add(tiles, d, sums):
        sums = list(sums)
        source = lax.rem(me + (n - d) * STEP, n)
        row = lax.rem(ty + ny - lax.div(source, nx), ny) * nx + lax.rem(tx + nx - lax.rem(source, nx), nx)
        for k in range(CAP):
            tile = tiles[d, k]
            t = jnp.full((NVAR, CELLS), goal_smem[row, k], jnp.int32)
            for j in range(TBD):
                sums[j] = sums[j] + jnp.where(t == j, tile, 0.0)
        return tuple(sums)

    def collect(b, sums):
        arrived(b, b * BATCH, BATCH).wait_recv()
        return lax.fori_loop(b * BATCH, (b + 1) * BATCH, functools.partial(add, got), sums)

    zero = jnp.zeros((NVAR, CELLS), jnp.float32)
    sums = add(send, 0, (zero,) * TBD)
    arrived(0, 1, BATCH - 1).wait_recv()
    sums = lax.fori_loop(1, BATCH, functools.partial(add, got), sums)
    sums = lax.fori_loop(1, n // BATCH, collect, sums)
    arrived(0, 1, n - 1).wait_send()
    for j in range(TBD):
        out_ref[j] = sums[j] / target_area_ref[j:j + 1, :]


def on_device(
    ny, nx,
    source_fields,
    diffusivity,
    cell_area,
    pair_block,
    pair_owner,
    pair_target,
    weight_blocks,
    target_area,
):
    n = ny * nx
    nvar, rows, cols = source_fields.shape
    pairs = weight_blocks.shape[0]
    vmem = pl.BlockSpec(memory_space=pltpu.VMEM)
    hbm = pl.BlockSpec(memory_space=pltpu.HBM)
    f32, i32 = jnp.float32, jnp.int32
    wide, tall = cols + 128, rows + 16
    sem = pltpu.SemaphoreType.DMA
    return pl.pallas_call(
        functools.partial(kernel, ny, nx),
        out_shape=jax.ShapeDtypeStruct((TBD, NVAR, CELLS), f32),
        in_specs=[hbm] * 8,
        out_specs=vmem,
        scratch_shapes=[
            pltpu.VMEM((rows, cols), f32),
            pltpu.VMEM((1, pairs), i32),
            pltpu.VMEM((1, pairs), i32),
            pltpu.VMEM((1, pairs), i32),
            pltpu.VMEM((TBD, CELLS), f32),
            pltpu.VMEM((nvar, tall, wide), f32),
            pltpu.VMEM((nvar, tall, wide), f32),
            pltpu.VMEM((tall, wide), f32),
            pltpu.VMEM((tall, wide), f32),
            pltpu.VMEM((tall, wide), f32),
            pltpu.VMEM((tall, wide), f32),
            pltpu.VMEM((tall, wide), f32),
            pltpu.VMEM((8 * FOLD, 128), f32),
            pltpu.VMEM((8 * FOLD + 16, 128), f32),
            pltpu.VMEM((8 * FOLD + 16, 128), f32),
            pltpu.VMEM((24, cols), f32),
            pltpu.VMEM((24, cols), f32),
            pltpu.VMEM((24, cols), f32),
            pltpu.VMEM((24, cols), f32),
            pltpu.VMEM((nvar * rows, 128), f32),
            pltpu.VMEM((nvar * rows, 128), f32),
            pltpu.VMEM((rows // BH * BCOL, NVAR, CELLS), f32),
            pltpu.VMEM((pairs, CELLS, CELLS), jnp.bfloat16),
            pltpu.VMEM((pairs, NVAR, CELLS), f32),
            pltpu.VMEM((n, CAP, NVAR, CELLS), f32),
            pltpu.VMEM((n, CAP, NVAR, CELLS), f32),
            pltpu.VMEM((8, pairs), i32),
            pltpu.SMEM((8, pairs), i32),
            pltpu.VMEM((n, 128), i32),
            pltpu.VMEM((n, 128), i32),
            pltpu.VMEM((n, 128), i32),
            pltpu.VMEM((n, 128), i32),
            pltpu.SMEM((n, 128), i32),
            sem((10,)),
            sem((4,)),
            sem((4,)),
            sem,
            sem((n // BATCH,)),
            sem((2,)),
            sem((2,)),
            pltpu.SemaphoreType.REGULAR,
        ],
        compiler_params=pltpu.CompilerParams(
            collective_id=0, has_side_effects=True, vmem_limit_bytes=62 * 1024 * 1024),
        name="regrid",
    )(
        source_fields, diffusivity, cell_area, pair_block.reshape(1, pairs), pair_owner.reshape(1, pairs),
        pair_target.reshape(1, pairs), weight_blocks, target_area,
    )


def solution(mesh):
    return jax.shard_map(
        functools.partial(on_device, mesh.shape["ty"], mesh.shape["tx"]),
        mesh=mesh,
        in_specs=(
            P(None, "ty", "tx"),
            P("ty", "tx"),
            P("ty", "tx"),
            P(("ty", "tx")),
            P(("ty", "tx"), None),
            P(("ty", "tx")),
            P(("ty", "tx"), None, None),
            P(("ty", "tx"), None),
        ),
        out_specs=P(("ty", "tx"), None, None),
        check_vma=False,
    )
```

```python
import functools

import jax
import jax.numpy as jnp
from jax import lax
from jax.experimental import pallas as pl
from jax.experimental.pallas import tpu as pltpu
from jax.sharding import PartitionSpec as P

NVAR = 8
BH = 8
BW = 16
BR = 12
BCOL = 16
TBD = 16
CAP = 4
CELLS = BH * BW
MESH = pl.DeviceIdType.MESH
STEP, BACK = 51, 123
GROUP = 16
SLOTS = GROUP // CAP
FOLD = 32
BATCH = 8
FIRST = 14
SECOND = 2
SIDE_FIRST, SIDE_SECOND = 49, 6


def kernel(
    ny, nx,
    fields_hbm, rate_hbm, area_hbm, block_hbm, owner_hbm, target_hbm, weight_hbm, target_area_hbm,
    out_ref,
    area_ref, block_ref, owner_ref, target_ref, target_area_ref,
    area_sides, stage, x0, x1, xe, y0, y1, ye, rate, k_east, k_north, pack, from_west, from_east,
    blocks, weights, part, send, got, tables, tables_smem, goal, relay, sorted_goal, goal_got, goal_smem,
    local_sem, edge_send, edge_recv, data_send, data_recv, goal_send, goal_recv, ready,
):
    n = ny * nx
    rows, cols = rate_hbm.shape
    pairs = weight_hbm.shape[0]
    total_rows = rows * ny
    ty, tx = lax.axis_index("ty"), lax.axis_index("tx")
    me = ty * nx + tx
    north, south = lax.rem(ty + 1, ny), lax.rem(ty + ny - 1, ny)
    east, west = lax.rem(tx + 1, nx), lax.rem(tx + nx - 1, nx)
    corners = [(north, east), (north, west), (south, east), (south, west)]

    entry = pltpu.get_barrier_semaphore()
    mates = [(ty, lax.rem(tx + d, nx)) for d in range(1, nx)]
    mates += [(lax.rem(ty + d, ny), tx) for d in range(1, ny)]
    mates += corners
    for mate in mates:
        pl.semaphore_signal(entry, inc=1, device_id=mate, device_id_type=MESH)

    own = slice(8, 8 + rows)
    loads = [
        (fields_hbm, stage),
        (rate_hbm.at[:, 0:128], rate.at[0, own]),
        (rate_hbm.at[:, 128:256], rate.at[1, own]),
        (block_hbm, block_ref),
        (owner_hbm, owner_ref),
        (target_hbm, target_ref),
        (area_hbm.at[:, 0:128], area_ref.at[0]),
        (area_hbm.at[:, 128:256], area_ref.at[1]),
        (target_area_hbm, target_area_ref),
        (weight_hbm, weights),
    ]
    loads = [pltpu.make_async_copy(src, dst, local_sem.at[i]) for i, (src, dst) in enumerate(loads)]
    for load in loads:
        load.start()
    for load in loads[:3]:
        load.wait()

    lane = lax.broadcasted_iota(jnp.int32, (8, 128), 1)
    xs, ys = (x0, x1), (y0, y1)

    def row(field, r):
        return field[pl.ds(pl.multiple_of(r * NVAR, NVAR), NVAR), :]

    def turn(i, carry):
        for v in range(NVAR):
            for t in range(2):
                tile = stage[v, pl.ds(pl.multiple_of(8 * i, 8), 8), 128 * t:128 * t + 128]
                xs[t][pl.ds((8 + 8 * i) * NVAR + v, 8, stride=NVAR), :] = tile
        return carry

    lax.fori_loop(0, rows // 8, turn, 0)

    def packed(firsts, lasts):
        total = jnp.zeros((8, 128), jnp.float32)
        for j, (first, last) in enumerate(zip(firsts, lasts)):
            edge = pltpu.roll(jnp.where(lane < 64, first, last), 4 * j + 2, 1)
            total = jnp.where((lane >= 4 * j) & (lane < 4 * j + 4), edge, total)
        return total

    for g, place in enumerate((0, 3, 2)):
        group = range(8 + FOLD * g, 8 + FOLD * (g + 1))
        pack[place] = packed([row(x0, r) for r in group], [row(x1, r) for r in group])
    group = range(8, 8 + rows, 8)
    pack[1] = packed([rate[0, r:r + 8, :] for r in group], [rate[1, r:r + 8, :] for r in group])

    pl.semaphore_wait(entry, len(mates))

    def edge_copy(i, src, dst, device):
        return pltpu.make_async_remote_copy(
            src_ref=src, dst_ref=dst, send_sem=edge_send.at[i], recv_sem=edge_recv.at[i],
            device_id=device, device_id_type=MESH)

    low, high = slice(6 * NVAR, 8 * NVAR), slice((8 + rows) * NVAR, (10 + rows) * NVAR)
    top, bottom = slice((6 + rows) * NVAR, (8 + rows) * NVAR), slice(8 * NVAR, 10 * NVAR)
    rate_low, rate_high = rate.at[0:2, 0:8], rate.at[0:2, 8 + rows:16 + rows]
    edges = [
        (0, pack.at[1:3], from_west.at[4:6], corners[0]),
        (1, pack.at[1:3], from_east.at[4:6], corners[1]),
        (0, pack.at[0:2], from_west.at[6:8], corners[2]),
        (1, pack.at[0:2], from_east.at[6:8], corners[3]),
        (0, pack, from_west.at[0:4], (ty, east)),
        (1, pack, from_east.at[0:4], (ty, west)),
        (2, x0.at[top], x0.at[low], (north, tx)),
        (3, x1.at[top], x1.at[low], (north, tx)),
        (4, rate.at[0:2, rows:8 + rows], rate_low, (north, tx)),
        (5, x0.at[bottom], x0.at[high], (south, tx)),
        (6, x1.at[bottom], x1.at[high], (south, tx)),
        (7, rate.at[0:2, 8:16], rate_high, (south, tx)),
    ]
    for edge in edges:
        edge_copy(*edge).start()
    for d in range(1, ny):
        pl.semaphore_signal(ready, inc=1, device_id=(lax.rem(ty + d, ny), tx), device_id_type=MESH)

    for load in loads[3:6]:
        load.wait()
    p_lane = lax.broadcasted_iota(jnp.int32, (1, pairs), 1)
    p_row = lax.broadcasted_iota(jnp.int32, (pairs, 1), 0)
    key_row = jnp.bitwise_and((owner_ref[...] - me + n) * BACK, n - 1)
    joint_row = p_lane * 4096 + block_ref[...] * TBD + target_ref[...]
    goal_row = target_ref[...] + 1
    eye = lax.broadcasted_iota(jnp.int32, (pairs, pairs), 0) == lax.broadcasted_iota(jnp.int32, (pairs, pairs), 1)

    def along(axis, mask, value):
        return jnp.sum(jnp.where(mask, value, 0), axis=axis, keepdims=True, dtype=jnp.int32)

    unique_row = key_row * pairs + p_lane
    key_col = along(1, eye, key_row)
    joint_col = along(1, eye, joint_row)
    unique_col = key_col * pairs + p_row
    place_row = along(0, unique_col < unique_row, 1)
    place_col = along(1, unique_row < unique_col, 1)
    joint = along(0, place_col == p_lane, joint_col)
    tables[0:1, :] = jnp.clip(lax.shift_right_logical(joint, 12), 0, pairs - 1)
    tables[1:2, :] = jnp.clip(jnp.bitwise_and(lax.shift_right_logical(joint, 4), 255), 0, blocks.shape[0] - 1)
    tables[2:3, :] = along(0, key_col < p_lane, 1)
    table_copy = pltpu.make_async_copy(tables, tables_smem, local_sem.at[10])
    table_copy.start()

    r_col = lax.broadcasted_iota(jnp.int32, (n, 1), 0)
    owner_col = lax.rem(r_col, ny) * nx + lax.div(r_col, ny)
    d_col = jnp.bitwise_and((owner_col - me + n) * BACK, n - 1)
    rank = jnp.where(key_row == d_col, place_row - along(1, key_row < d_col, 1), -1)
    d_lane = lax.broadcasted_iota(jnp.int32, (n, 128), 1)
    goals = jnp.zeros((n, 128), jnp.int32)
    for k in range(CAP):
        goals = jnp.where(d_lane == k, along(1, rank == k, goal_row), goals)
    goal[...] = goals - 1

    def rows_of(i, size):
        return pl.ds(pl.multiple_of(i * size, 8), size)

    def goal_copy(i, src, dst, device):
        return pltpu.make_async_remote_copy(
            src_ref=src, dst_ref=dst, send_sem=goal_send.at[i], recv_sem=goal_recv.at[i],
            device_id=device, device_id_type=MESH)

    along_tx, along_ty = [], []
    for d in range(1, nx):
        to = lax.rem(tx + d, nx)
        along_tx.append(goal_copy(0, goal.at[rows_of(to, ny)], relay.at[d * ny:(d + 1) * ny], (ty, to)))
    for d in range(1, ny):
        to = lax.rem(ty + d, ny)
        along_ty.append(goal_copy(1, sorted_goal.at[rows_of(to, nx)], goal_got.at[d * nx:(d + 1) * nx], (to, tx)))
    for copy in along_tx:
        copy.start()
    relay[0:ny, :] = goal[rows_of(tx, ny), :]

    sub = lax.broadcasted_iota(jnp.int32, (8, 128), 0)
    inner = (rows + 8) // 8
    bands = inner + 1

    def from_next(tiles):
        moved = [pltpu.roll(c, 127, 1) for c in tiles]
        if len(tiles) == 1:
            return moved
        return [jnp.where(lane < 127, moved[t], moved[1 - t]) for t in range(2)]

    def from_previous(tiles):
        moved = [pltpu.roll(c, 1, 1) for c in tiles]
        if len(tiles) == 1:
            return moved
        return [jnp.where(lane > 0, moved[t], moved[1 - t]) for t in range(2)]

    def rate_band(tiles, i, last):
        here, above = [[rate[t, 8 * b:8 * b + 8, :] for t in tiles] for b in (i, min(i + 1, last))]
        g = sub + (ty * rows + 8 * i - 8)
        inside = (g >= 0) & (g < total_rows - 1)
        for t, c, n_value, e in zip(tiles, here, above, from_next(here)):
            n_value = jnp.where(sub < 7, pltpu.roll(c, 7, 0), pltpu.roll(n_value, 7, 0))
            k_east[t, 8 * i:8 * i + 8, :] = 0.5 * (c + e)
            k_north[t, 8 * i:8 * i + 8, :] = jnp.where(inside, 0.5 * (c + n_value), 0.0)

    def north_flux(t, r, c, n_value):
        return k_north[t, pl.ds(r, 1), :] * (n_value - c)

    def advance(fields, tiles, r, c, below):
        above = [row(field, r + 1) for field in fields]
        flux = [north_flux(t, r, *pair) for t, pair in zip(tiles, zip(c, above))]
        side = [k_east[t, pl.ds(r, 1), :] * (e - p) for t, p, e in zip(tiles, c, from_next(c))]
        back = from_previous(side)
        return above, flux, [p + a - b + f - q for p, a, b, f, q in zip(c, side, back, flux, below)]

    def begin_at(fields, tiles, r):
        c = [row(field, r) for field in fields]
        return c, [north_flux(t, r - 1, row(field, r - 1), p) for t, field, p in zip(tiles, fields, c)]

    def first_pass(fields, results, tiles, start, count, carry):
        for u in range(count):
            *carry, z = advance(fields, tiles, start + u, *carry)
            for result, p in zip(results, z):
                result[pl.ds(pl.multiple_of((start + u) * NVAR, NVAR), NVAR), :] = p
        return tuple(carry)

    def second_pass(fields, tiles, block, carry):
        out = []
        for j in range(BH):
            *carry, z = advance(fields, tiles, 8 + block * BH + j, *carry)
            out.append(z)
        return tuple(carry), out

    def whole_blocks(block, carry):
        carry, out = second_pass(ys, (0, 1), block, carry)
        for t in range(2):
            tile = [area_ref[t, pl.ds(block * BH + j, 1), :] * z[t] for j, z in enumerate(out)]
            for bit in (1, 2, 4):
                mask = jnp.bitwise_and(lane, 16 * bit) == 0
                for j in range(BH):
                    if j & bit:
                        continue
                    lo, hi = tile[j], tile[j + bit]
                    tile[j] = jnp.where(mask, lo, pltpu.roll(hi, 16 * bit, 1))
                    tile[j + bit] = jnp.where(mask, pltpu.roll(lo, 128 - 16 * bit, 1), hi)
            for j in range(BH):
                blocks[block * BCOL + t * BH + j] = tile[j]
        return carry

    for i in range(1, inner):
        rate_band((0, 1), i, inner - 1)
    block_rows = rows // BH
    every_row = lambda r: jnp.where(lane < 60, row(x0, r), pltpu.roll(row(x1, r), 124, 1))

    def inside_first(b, carry):
        for u in range(FIRST):
            r = 14 + b * FIRST + u
            xe[pl.ds(pl.multiple_of(r * NVAR, NVAR), NVAR), :] = every_row(r)
        return first_pass(xs, ys, (0, 1), 14 + b * FIRST, FIRST, carry)

    lax.fori_loop(0, (rows - 12) // FIRST, inside_first, begin_at(xs, (0, 1), 14))
    for load in loads[6:8]:
        load.wait()

    def inside_second(b, carry):
        for u in range(SECOND):
            carry = whole_blocks(1 + b * SECOND + u, carry)
        return carry

    lax.fori_loop(0, (block_rows - 2) // SECOND, inside_second, begin_at(ys, (0, 1), 16))

    for block in range(block_rows):
        for t, base in enumerate((0, 112)):
            total = jnp.zeros((1, 128), jnp.float32)
            for j in range(BH):
                moved = pltpu.roll(jnp.broadcast_to(area_ref[t, block * BH + j:block * BH + j + 1, :], (8, 128)), (16 * j - base) % 128, 1)
                total = jnp.where(lax.shift_right_logical(lane[0:1], 4) == j, moved[0:1], total)
            area_sides[t, block:block + 1, :] = total

    landing = (from_west, from_east, x0.at[low], x1.at[low], rate_low, x0.at[high], x1.at[high], rate_high)
    for i, landed in enumerate(landing):
        edge_copy(i, landed, landed, (ty, east)).wait()

    for i in (0, inner - 1, inner):
        rate_band((0, 1), i, inner)

    def ends(side, carry):
        start = 7 + side * (rows - 5)
        first_pass(xs, ys, (0, 1), start, 7, begin_at(xs, (0, 1), start))
        return carry

    ends(0, 0)
    ends(1, 0)

    def end_blocks(side, carry):
        block = side * (block_rows - 1)
        whole_blocks(block, begin_at(ys, (0, 1), 8 + block * BH))
        return carry

    end_blocks(0, 0)
    end_blocks(1, 0)

    both = []
    for i in range(8):
        both.append(jnp.where(jnp.bitwise_and(lane, 3) < 2, pltpu.roll(from_east[i], 126, 1), pltpu.roll(from_west[i], 2, 1)))

    def opened(tile, j):
        return pltpu.roll(tile, 124 - 4 * j, 1) if j < 31 else tile

    def put(r, tile, j):
        own_part = xe[NVAR * r:NVAR * r + NVAR, :] if 14 <= r < 2 + rows else every_row(r)
        xe[NVAR * r:NVAR * r + NVAR, :] = jnp.where(lane < 124, own_part, opened(tile, j))

    for g, place in enumerate((0, 3, 2)):
        for j in range(FOLD):
            put(8 + FOLD * g + j, both[place], j)
    put(7, both[5], FOLD - 1)
    put(8 + rows, both[6], 0)
    for r in (6, 9 + rows):
        xe[NVAR * r:NVAR * r + NVAR, :] = every_row(r)
    for i in range(bands):
        if i == 0:
            side = opened(both[4], rows // 8 - 1)
        elif i == inner:
            side = opened(both[7], 0)
        else:
            side = opened(both[1], i - 1)
        own_part = jnp.where(lane < 60, rate[0, 8 * i:8 * i + 8, :], pltpu.roll(rate[1, 8 * i:8 * i + 8, :], 124, 1))
        rate[2, 8 * i:8 * i + 8, :] = jnp.where(lane < 124, own_part, side)
    for i in range(bands):
        rate_band((2,), i, inner)

    def side_first(b, carry):
        return first_pass((xe,), (ye,), (2,), 7 + b * SIDE_FIRST, SIDE_FIRST, carry)

    lax.fori_loop(0, (rows + 2) // SIDE_FIRST, side_first, begin_at((xe,), (2,), 7))

    def side_second(b, carry):
        for u in range(SIDE_SECOND):
            block = b * SIDE_SECOND + u
            carry, out = second_pass((ye,), (2,), block, carry)
            left, right = None, None
            for j, (z,) in enumerate(out):
                l_value = pltpu.roll(z, 16 * j, 1) if j else z
                r_value = pltpu.roll(z, (16 * j + 20) % 128, 1)
                here = lax.shift_right_logical(lane, 4) == j
                left = l_value if j == 0 else jnp.where(here, l_value, left)
                right = r_value if j == 0 else jnp.where(here, r_value, right)
            blocks[block * BCOL] = left * area_sides[0, pl.ds(block, 1), :]
            blocks[block * BCOL + BCOL - 1] = right * area_sides[1, pl.ds(block, 1), :]
        return carry

    lax.fori_loop(0, block_rows // SIDE_SECOND, side_second, begin_at((ye,), (2,), 8))

    def peer(d):
        p = lax.rem(me + lax.rem(d * STEP, n), n)
        return (p // nx, lax.rem(p, nx))

    def data_copy(d):
        return pltpu.make_async_remote_copy(
            src_ref=send.at[d], dst_ref=got.at[d], send_sem=data_send,
            recv_sem=data_recv.at[lax.div(d, BATCH)], device_id=peer(d), device_id_type=MESH)

    def every(start, stop, action):
        def body(d, carry):
            action(d)
            return carry
        lax.fori_loop(start, stop, body, 0)

    table_copy.wait()
    for load in loads[8:]:
        load.wait()

    def multiply(q):
        for u in range(GROUP):
            i = q * GROUP + u
            a = blocks[tables_smem[1, i]].astype(jnp.bfloat16)
            part[i] = jnp.dot(a, weights[tables_smem[0, i]], preferred_element_type=jnp.float32)

    def fill(q):
        for u in range(SLOTS):
            d = q * SLOTS + u
            first = tables_smem[2, d]
            for k in range(CAP):
                send[d, k] = part[jnp.minimum(first + k, pairs - 1)]

    def launch(q):
        for u in range(SLOTS):
            data_copy(q * SLOTS + u).start()

    last = n // SLOTS
    groups = pairs // GROUP
    multiply(0)
    fill(0)
    multiply(1)
    pl.semaphore_wait(ready, ny - 1)
    for u in range(1, SLOTS):
        data_copy(u).start()
    fill(1)
    multiply(2)

    landed = relay.at[ny:n]
    goal_copy(0, landed, landed, (ty, east)).wait()
    for i in range(ny):
        sorted_goal[i * nx:(i + 1) * nx, :] = relay[pl.ds(i, nx, stride=ny), :]
    goal_got[0:nx, :] = sorted_goal[rows_of(ty, nx), :]
    launch(1)
    fill(2)
    multiply(3)
    for copy in along_ty:
        copy.start()

    def busy(q):
        launch(q - 2)
        fill(q - 1)
        multiply(q)

    def rest(q):
        launch(q - 2)
        fill(q - 1)

    every(4, groups, busy)
    every(groups, last + 1, rest)
    launch(last - 1)

    landed = goal_got.at[nx:n]
    goal_copy(1, landed, landed, (north, tx)).wait()
    goal_table = pltpu.make_async_copy(goal_got, goal_smem, local_sem.at[11])
    goal_table.start()
    goal_table.wait()

    def arrived(b, start, size):
        landed = got.at[pl.ds(start, size)]
        return pltpu.make_async_remote_copy(
            src_ref=landed, dst_ref=landed, send_sem=data_send, recv_sem=data_recv.at[b],
            device_id=(ty, east), device_id_type=MESH)

    def add(tiles, d, sums):
        sums = list(sums)
        source = lax.rem(me + (n - d) * STEP, n)
        row = lax.rem(ty + ny - lax.div(source, nx), ny) * nx + lax.rem(tx + nx - lax.rem(source, nx), nx)
        for k in range(CAP):
            tile = tiles[d, k]
            t = jnp.full((NVAR, CELLS), goal_smem[row, k], jnp.int32)
            for j in range(TBD):
                sums[j] = sums[j] + jnp.where(t == j, tile, 0.0)
        return tuple(sums)

    def collect(b, sums):
        arrived(b, b * BATCH, BATCH).wait_recv()
        return lax.fori_loop(b * BATCH, (b + 1) * BATCH, functools.partial(add, got), sums)

    zero = jnp.zeros((NVAR, CELLS), jnp.float32)
    sums = add(send, 0, (zero,) * TBD)
    arrived(0, 1, BATCH - 1).wait_recv()
    sums = lax.fori_loop(1, BATCH, functools.partial(add, got), sums)
    sums = lax.fori_loop(1, n // BATCH, collect, sums)
    arrived(0, 1, n - 1).wait_send()
    for j in range(TBD):
        out_ref[j] = sums[j] / target_area_ref[j:j + 1, :]


def on_device(
    ny, nx,
    source_fields,
    diffusivity,
    cell_area,
    pair_block,
    pair_owner,
    pair_target,
    weight_blocks,
    target_area,
):
    n = ny * nx
    nvar, rows, cols = source_fields.shape
    pairs = weight_blocks.shape[0]
    vmem = pl.BlockSpec(memory_space=pltpu.VMEM)
    hbm = pl.BlockSpec(memory_space=pltpu.HBM)
    f32, i32 = jnp.float32, jnp.int32
    tall = rows + 16
    sem = pltpu.SemaphoreType.DMA
    return pl.pallas_call(
        functools.partial(kernel, ny, nx),
        out_shape=jax.ShapeDtypeStruct((TBD, NVAR, CELLS), f32),
        in_specs=[hbm] * 8,
        out_specs=vmem,
        scratch_shapes=[
            pltpu.VMEM((2, rows, 128), f32),
            pltpu.VMEM((1, pairs), i32),
            pltpu.VMEM((1, pairs), i32),
            pltpu.VMEM((1, pairs), i32),
            pltpu.VMEM((TBD, CELLS), f32),
            pltpu.VMEM((2, 16, 128), f32),
            pltpu.VMEM((nvar, rows, cols), f32),
            pltpu.VMEM((tall * nvar, 128), f32),
            pltpu.VMEM((tall * nvar, 128), f32),
            pltpu.VMEM((tall * nvar, 128), f32),
            pltpu.VMEM((tall * nvar, 128), f32),
            pltpu.VMEM((tall * nvar, 128), f32),
            pltpu.VMEM((tall * nvar, 128), f32),
            pltpu.VMEM((3, tall, 128), f32),
            pltpu.VMEM((3, tall, 128), f32),
            pltpu.VMEM((3, tall, 128), f32),
            pltpu.VMEM((4, 8, 128), f32),
            pltpu.VMEM((8, 8, 128), f32),
            pltpu.VMEM((8, 8, 128), f32),
            pltpu.VMEM((rows // BH * BCOL, NVAR, CELLS), f32),
            pltpu.VMEM((pairs, CELLS, CELLS), jnp.bfloat16),
            pltpu.VMEM((pairs, NVAR, CELLS), f32),
            pltpu.VMEM((n, CAP, NVAR, CELLS), f32),
            pltpu.VMEM((n, CAP, NVAR, CELLS), f32),
            pltpu.VMEM((8, pairs), i32),
            pltpu.SMEM((8, pairs), i32),
            pltpu.VMEM((n, 128), i32),
            pltpu.VMEM((n, 128), i32),
            pltpu.VMEM((n, 128), i32),
            pltpu.VMEM((n, 128), i32),
            pltpu.SMEM((n, 128), i32),
            sem((12,)),
            sem((8,)),
            sem((8,)),
            sem,
            sem((n // BATCH,)),
            sem((2,)),
            sem((2,)),
            pltpu.SemaphoreType.REGULAR,
        ],
        compiler_params=pltpu.CompilerParams(
            collective_id=0, has_side_effects=True, vmem_limit_bytes=62 * 1024 * 1024),
        name="regrid",
    )(
        source_fields, diffusivity, cell_area, pair_block.reshape(1, pairs), pair_owner.reshape(1, pairs),
        pair_target.reshape(1, pairs), weight_blocks, target_area,
    )


def solution(mesh):
    return jax.shard_map(
        functools.partial(on_device, mesh.shape["ty"], mesh.shape["tx"]),
        mesh=mesh,
        in_specs=(
            P(None, "ty", "tx"),
            P("ty", "tx"),
            P("ty", "tx"),
            P(("ty", "tx")),
            P(("ty", "tx"), None),
            P(("ty", "tx")),
            P(("ty", "tx"), None, None),
            P(("ty", "tx"), None),
        ),
        out_specs=P(("ty", "tx"), None, None),
        check_vma=False,
    )
```

```python
import functools

import jax
import jax.numpy as jnp
from jax import lax
from jax.experimental import pallas as pl
from jax.experimental.pallas import tpu as pltpu
from jax.sharding import PartitionSpec as P

NVAR = 8
BH = 8
BW = 16
BR = 12
BCOL = 16
TBD = 16
CAP = 4
CELLS = BH * BW
MESH = pl.DeviceIdType.MESH
STEP, BACK = 43, 3
GROUP = 16
SLOTS = GROUP // CAP
FOLD = 32
BATCH = 8
FIRST = 14
SECOND = 2
SIDE_FIRST, SIDE_SECOND = 49, 6


def kernel(
    ny, nx,
    fields_hbm, rate_hbm, area_hbm, block_hbm, owner_hbm, target_hbm, weight_hbm, target_area_hbm,
    out_ref,
    area_ref, block_ref, owner_ref, target_ref, target_area_ref,
    area_sides, stage, x0, x1, xe, y0, y1, ye, rate, k_east, k_north, pack, from_west, from_east,
    blocks, weights, part, send, got, tables, tables_smem, goal, relay, sorted_goal, goal_got, goal_smem,
    local_sem, edge_send, edge_recv, data_send, data_recv, goal_send, goal_recv, ready,
):
    n = ny * nx
    rows, cols = rate_hbm.shape
    pairs = weight_hbm.shape[0]
    total_rows = rows * ny
    ty, tx = lax.axis_index("ty"), lax.axis_index("tx")
    me = ty * nx + tx
    north, south = lax.rem(ty + 1, ny), lax.rem(ty + ny - 1, ny)
    east, west = lax.rem(tx + 1, nx), lax.rem(tx + nx - 1, nx)
    corners = [(north, east), (north, west), (south, east), (south, west)]

    entry = pltpu.get_barrier_semaphore()
    mates = [(ty, lax.rem(tx + d, nx)) for d in range(1, nx)]
    mates += [(lax.rem(ty + d, ny), tx) for d in range(1, ny)]
    mates += corners
    for mate in mates:
        pl.semaphore_signal(entry, inc=1, device_id=mate, device_id_type=MESH)

    own = slice(8, 8 + rows)
    loads = [
        (fields_hbm, stage),
        (rate_hbm.at[:, 0:128], rate.at[0, own]),
        (rate_hbm.at[:, 128:256], rate.at[1, own]),
        (block_hbm, block_ref),
        (owner_hbm, owner_ref),
        (target_hbm, target_ref),
        (area_hbm.at[:, 0:128], area_ref.at[0]),
        (area_hbm.at[:, 128:256], area_ref.at[1]),
        (target_area_hbm, target_area_ref),
        (weight_hbm, weights),
    ]
    loads = [pltpu.make_async_copy(src, dst, local_sem.at[i]) for i, (src, dst) in enumerate(loads)]
    for load in loads:
        load.start()
    for load in loads[:3]:
        load.wait()

    lane = lax.broadcasted_iota(jnp.int32, (8, 128), 1)
    xs, ys = (x0, x1), (y0, y1)

    def row(field, r):
        return field[pl.ds(pl.multiple_of(r * NVAR, NVAR), NVAR), :]

    def turn(i, carry):
        for v in range(NVAR):
            for t in range(2):
                tile = stage[v, pl.ds(pl.multiple_of(8 * i, 8), 8), 128 * t:128 * t + 128]
                xs[t][pl.ds((8 + 8 * i) * NVAR + v, 8, stride=NVAR), :] = tile
        return carry

    lax.fori_loop(0, rows // 8, turn, 0)

    def packed(firsts, lasts):
        total = jnp.zeros((8, 128), jnp.float32)
        for j, (first, last) in enumerate(zip(firsts, lasts)):
            edge = pltpu.roll(jnp.where(lane < 64, first, last), 4 * j + 2, 1)
            total = jnp.where((lane >= 4 * j) & (lane < 4 * j + 4), edge, total)
        return total

    for g, place in enumerate((0, 3, 2)):
        group = range(8 + FOLD * g, 8 + FOLD * (g + 1))
        pack[place] = packed([row(x0, r) for r in group], [row(x1, r) for r in group])
    group = range(8, 8 + rows, 8)
    pack[1] = packed([rate[0, r:r + 8, :] for r in group], [rate[1, r:r + 8, :] for r in group])

    pl.semaphore_wait(entry, len(mates))

    def edge_copy(i, src, dst, device):
        return pltpu.make_async_remote_copy(
            src_ref=src, dst_ref=dst, send_sem=edge_send.at[i], recv_sem=edge_recv.at[i],
            device_id=device, device_id_type=MESH)

    low, high = slice(6 * NVAR, 8 * NVAR), slice((8 + rows) * NVAR, (10 + rows) * NVAR)
    top, bottom = slice((6 + rows) * NVAR, (8 + rows) * NVAR), slice(8 * NVAR, 10 * NVAR)
    rate_low, rate_high = rate.at[0:2, 0:8], rate.at[0:2, 8 + rows:16 + rows]
    edges = [
        (0, pack.at[1:3], from_west.at[4:6], corners[0]),
        (1, pack.at[1:3], from_east.at[4:6], corners[1]),
        (0, pack.at[0:2], from_west.at[6:8], corners[2]),
        (1, pack.at[0:2], from_east.at[6:8], corners[3]),
        (0, pack, from_west.at[0:4], (ty, east)),
        (1, pack, from_east.at[0:4], (ty, west)),
        (2, x0.at[top], x0.at[low], (north, tx)),
        (3, x1.at[top], x1.at[low], (north, tx)),
        (4, rate.at[0:2, rows:8 + rows], rate_low, (north, tx)),
        (5, x0.at[bottom], x0.at[high], (south, tx)),
        (6, x1.at[bottom], x1.at[high], (south, tx)),
        (7, rate.at[0:2, 8:16], rate_high, (south, tx)),
    ]
    for edge in edges:
        edge_copy(*edge).start()
    for d in range(1, ny):
        pl.semaphore_signal(ready, inc=1, device_id=(lax.rem(ty + d, ny), tx), device_id_type=MESH)

    for load in loads[3:6]:
        load.wait()
    p_lane = lax.broadcasted_iota(jnp.int32, (1, pairs), 1)
    p_row = lax.broadcasted_iota(jnp.int32, (pairs, 1), 0)
    key_row = jnp.bitwise_and((owner_ref[...] - me + n) * BACK, n - 1)
    joint_row = p_lane * 4096 + block_ref[...] * TBD + target_ref[...]
    goal_row = target_ref[...] + 1
    eye = lax.broadcasted_iota(jnp.int32, (pairs, pairs), 0) == lax.broadcasted_iota(jnp.int32, (pairs, pairs), 1)

    def along(axis, mask, value):
        return jnp.sum(jnp.where(mask, value, 0), axis=axis, keepdims=True, dtype=jnp.int32)

    unique_row = key_row * pairs + p_lane
    key_col = along(1, eye, key_row)
    joint_col = along(1, eye, joint_row)
    unique_col = key_col * pairs + p_row
    place_row = along(0, unique_col < unique_row, 1)
    place_col = along(1, unique_row < unique_col, 1)
    joint = along(0, place_col == p_lane, joint_col)
    tables[0:1, :] = jnp.clip(lax.shift_right_logical(joint, 12), 0, pairs - 1)
    tables[1:2, :] = jnp.clip(jnp.bitwise_and(lax.shift_right_logical(joint, 4), 255), 0, blocks.shape[0] - 1)
    tables[2:3, :] = along(0, key_col < p_lane, 1)
    table_copy = pltpu.make_async_copy(tables, tables_smem, local_sem.at[10])
    table_copy.start()

    r_col = lax.broadcasted_iota(jnp.int32, (n, 1), 0)
    owner_col = lax.rem(r_col, ny) * nx + lax.div(r_col, ny)
    d_col = jnp.bitwise_and((owner_col - me + n) * BACK, n - 1)
    rank = jnp.where(key_row == d_col, place_row - along(1, key_row < d_col, 1), -1)
    d_lane = lax.broadcasted_iota(jnp.int32, (n, 128), 1)
    goals = jnp.zeros((n, 128), jnp.int32)
    for k in range(CAP):
        goals = jnp.where(d_lane == k, along(1, rank == k, goal_row), goals)
    goal[...] = goals - 1

    def rows_of(i, size):
        return pl.ds(pl.multiple_of(i * size, 8), size)

    def goal_copy(i, src, dst, device):
        return pltpu.make_async_remote_copy(
            src_ref=src, dst_ref=dst, send_sem=goal_send.at[i], recv_sem=goal_recv.at[i],
            device_id=device, device_id_type=MESH)

    along_tx, along_ty = [], []
    for d in range(1, nx):
        to = lax.rem(tx + d, nx)
        along_tx.append(goal_copy(0, goal.at[rows_of(to, ny)], relay.at[d * ny:(d + 1) * ny], (ty, to)))
    for d in range(1, ny):
        to = lax.rem(ty + d, ny)
        along_ty.append(goal_copy(1, sorted_goal.at[rows_of(to, nx)], goal_got.at[d * nx:(d + 1) * nx], (to, tx)))
    for copy in along_tx:
        copy.start()
    relay[0:ny, :] = goal[rows_of(tx, ny), :]

    sub = lax.broadcasted_iota(jnp.int32, (8, 128), 0)
    inner = (rows + 8) // 8
    bands = inner + 1

    def from_next(tiles):
        moved = [pltpu.roll(c, 127, 1) for c in tiles]
        if len(tiles) == 1:
            return moved
        return [jnp.where(lane < 127, moved[t], moved[1 - t]) for t in range(2)]

    def from_previous(tiles):
        moved = [pltpu.roll(c, 1, 1) for c in tiles]
        if len(tiles) == 1:
            return moved
        return [jnp.where(lane > 0, moved[t], moved[1 - t]) for t in range(2)]

    def rate_band(tiles, i, last):
        here, above = [[rate[t, 8 * b:8 * b + 8, :] for t in tiles] for b in (i, min(i + 1, last))]
        g = sub + (ty * rows + 8 * i - 8)
        inside = (g >= 0) & (g < total_rows - 1)
        for t, c, n_value, e in zip(tiles, here, above, from_next(here)):
            n_value = jnp.where(sub < 7, pltpu.roll(c, 7, 0), pltpu.roll(n_value, 7, 0))
            k_east[t, 8 * i:8 * i + 8, :] = 0.5 * (c + e)
            k_north[t, 8 * i:8 * i + 8, :] = jnp.where(inside, 0.5 * (c + n_value), 0.0)

    def north_flux(t, r, c, n_value):
        return k_north[t, pl.ds(r, 1), :] * (n_value - c)

    def advance(fields, tiles, r, c, below):
        above = [row(field, r + 1) for field in fields]
        flux = [north_flux(t, r, *pair) for t, pair in zip(tiles, zip(c, above))]
        side = [k_east[t, pl.ds(r, 1), :] * (e - p) for t, p, e in zip(tiles, c, from_next(c))]
        back = from_previous(side)
        return above, flux, [p + a - b + f - q for p, a, b, f, q in zip(c, side, back, flux, below)]

    def begin_at(fields, tiles, r):
        c = [row(field, r) for field in fields]
        return c, [north_flux(t, r - 1, row(field, r - 1), p) for t, field, p in zip(tiles, fields, c)]

    def first_pass(fields, results, tiles, start, count, carry):
        for u in range(count):
            *carry, z = advance(fields, tiles, start + u, *carry)
            for result, p in zip(results, z):
                result[pl.ds(pl.multiple_of((start + u) * NVAR, NVAR), NVAR), :] = p
        return tuple(carry)

    def second_pass(fields, tiles, block, carry):
        out = []
        for j in range(BH):
            *carry, z = advance(fields, tiles, 8 + block * BH + j, *carry)
            out.append(z)
        return tuple(carry), out

    def whole_blocks(block, carry):
        carry, out = second_pass(ys, (0, 1), block, carry)
        for t in range(2):
            tile = [area_ref[t, pl.ds(block * BH + j, 1), :] * z[t] for j, z in enumerate(out)]
            for bit in (1, 2, 4):
                mask = jnp.bitwise_and(lane, 16 * bit) == 0
                for j in range(BH):
                    if j & bit:
                        continue
                    lo, hi = tile[j], tile[j + bit]
                    tile[j] = jnp.where(mask, lo, pltpu.roll(hi, 16 * bit, 1))
                    tile[j + bit] = jnp.where(mask, pltpu.roll(lo, 128 - 16 * bit, 1), hi)
            for j in range(BH):
                blocks[block * BCOL + t * BH + j] = tile[j]
        return carry

    for i in range(1, inner):
        rate_band((0, 1), i, inner - 1)
    block_rows = rows // BH
    every_row = lambda r: jnp.where(lane < 60, row(x0, r), pltpu.roll(row(x1, r), 124, 1))

    def inside_first(b, carry):
        for u in range(FIRST):
            r = 14 + b * FIRST + u
            xe[pl.ds(pl.multiple_of(r * NVAR, NVAR), NVAR), :] = every_row(r)
        return first_pass(xs, ys, (0, 1), 14 + b * FIRST, FIRST, carry)

    lax.fori_loop(0, (rows - 12) // FIRST, inside_first, begin_at(xs, (0, 1), 14))
    for load in loads[6:8]:
        load.wait()

    def inside_second(b, carry):
        for u in range(SECOND):
            carry = whole_blocks(1 + b * SECOND + u, carry)
        return carry

    lax.fori_loop(0, (block_rows - 2) // SECOND, inside_second, begin_at(ys, (0, 1), 16))

    for block in range(block_rows):
        for t, base in enumerate((0, 112)):
            total = jnp.zeros((1, 128), jnp.float32)
            for j in range(BH):
                moved = pltpu.roll(jnp.broadcast_to(area_ref[t, block * BH + j:block * BH + j + 1, :], (8, 128)), (16 * j - base) % 128, 1)
                total = jnp.where(lax.shift_right_logical(lane[0:1], 4) == j, moved[0:1], total)
            area_sides[t, block:block + 1, :] = total

    landing = (from_west, from_east, x0.at[low], x1.at[low], rate_low, x0.at[high], x1.at[high], rate_high)
    for i, landed in enumerate(landing):
        edge_copy(i, landed, landed, (ty, east)).wait()

    for i in (0, inner - 1, inner):
        rate_band((0, 1), i, inner)

    def ends(side, carry):
        start = 7 + side * (rows - 5)
        first_pass(xs, ys, (0, 1), start, 7, begin_at(xs, (0, 1), start))
        return carry

    ends(0, 0)
    ends(1, 0)

    def end_blocks(side, carry):
        block = side * (block_rows - 1)
        whole_blocks(block, begin_at(ys, (0, 1), 8 + block * BH))
        return carry

    end_blocks(0, 0)
    end_blocks(1, 0)

    both = []
    for i in range(8):
        both.append(jnp.where(jnp.bitwise_and(lane, 3) < 2, pltpu.roll(from_east[i], 126, 1), pltpu.roll(from_west[i], 2, 1)))

    def opened(tile, j):
        return pltpu.roll(tile, 124 - 4 * j, 1) if j < 31 else tile

    def put(r, tile, j):
        own_part = xe[NVAR * r:NVAR * r + NVAR, :] if 14 <= r < 2 + rows else every_row(r)
        xe[NVAR * r:NVAR * r + NVAR, :] = jnp.where(lane < 124, own_part, opened(tile, j))

    for g, place in enumerate((0, 3, 2)):
        for j in range(FOLD):
            put(8 + FOLD * g + j, both[place], j)
    put(7, both[5], FOLD - 1)
    put(8 + rows, both[6], 0)
    for r in (6, 9 + rows):
        xe[NVAR * r:NVAR * r + NVAR, :] = every_row(r)
    for i in range(bands):
        if i == 0:
            side = opened(both[4], rows // 8 - 1)
        elif i == inner:
            side = opened(both[7], 0)
        else:
            side = opened(both[1], i - 1)
        own_part = jnp.where(lane < 60, rate[0, 8 * i:8 * i + 8, :], pltpu.roll(rate[1, 8 * i:8 * i + 8, :], 124, 1))
        rate[2, 8 * i:8 * i + 8, :] = jnp.where(lane < 124, own_part, side)
    for i in range(bands):
        rate_band((2,), i, inner)

    def side_first(b, carry):
        return first_pass((xe,), (ye,), (2,), 7 + b * SIDE_FIRST, SIDE_FIRST, carry)

    lax.fori_loop(0, (rows + 2) // SIDE_FIRST, side_first, begin_at((xe,), (2,), 7))

    def side_second(b, carry):
        for u in range(SIDE_SECOND):
            block = b * SIDE_SECOND + u
            carry, out = second_pass((ye,), (2,), block, carry)
            left, right = None, None
            for j, (z,) in enumerate(out):
                l_value = pltpu.roll(z, 16 * j, 1) if j else z
                r_value = pltpu.roll(z, (16 * j + 20) % 128, 1)
                here = lax.shift_right_logical(lane, 4) == j
                left = l_value if j == 0 else jnp.where(here, l_value, left)
                right = r_value if j == 0 else jnp.where(here, r_value, right)
            blocks[block * BCOL] = left * area_sides[0, pl.ds(block, 1), :]
            blocks[block * BCOL + BCOL - 1] = right * area_sides[1, pl.ds(block, 1), :]
        return carry

    lax.fori_loop(0, block_rows // SIDE_SECOND, side_second, begin_at((ye,), (2,), 8))

    def peer(d):
        p = lax.rem(me + lax.rem(d * STEP, n), n)
        return (p // nx, lax.rem(p, nx))

    def data_copy(d):
        return pltpu.make_async_remote_copy(
            src_ref=send.at[d], dst_ref=got.at[d], send_sem=data_send,
            recv_sem=data_recv.at[lax.div(d, BATCH)], device_id=peer(d), device_id_type=MESH)

    def every(start, stop, action):
        def body(d, carry):
            action(d)
            return carry
        lax.fori_loop(start, stop, body, 0)

    table_copy.wait()
    for load in loads[8:]:
        load.wait()

    def multiply(q):
        for u in range(GROUP):
            i = q * GROUP + u
            a = blocks[tables_smem[1, i]].astype(jnp.bfloat16)
            part[i] = jnp.dot(a, weights[tables_smem[0, i]], preferred_element_type=jnp.float32)

    def fill(q):
        for u in range(SLOTS):
            d = q * SLOTS + u
            first = tables_smem[2, d]
            for k in range(CAP):
                send[d, k] = part[jnp.minimum(first + k, pairs - 1)]

    def launch(q):
        for u in range(SLOTS):
            data_copy(q * SLOTS + u).start()

    last = n // SLOTS
    groups = pairs // GROUP
    multiply(0)
    fill(0)
    multiply(1)
    pl.semaphore_wait(ready, ny - 1)
    for u in range(1, SLOTS):
        data_copy(u).start()
    fill(1)
    multiply(2)

    landed = relay.at[ny:n]
    goal_copy(0, landed, landed, (ty, east)).wait()
    for i in range(ny):
        sorted_goal[i * nx:(i + 1) * nx, :] = relay[pl.ds(i, nx, stride=ny), :]
    goal_got[0:nx, :] = sorted_goal[rows_of(ty, nx), :]
    launch(1)
    fill(2)
    multiply(3)
    for copy in along_ty:
        copy.start()

    def busy(q):
        launch(q - 2)
        fill(q - 1)
        multiply(q)

    def rest(q):
        launch(q - 2)
        fill(q - 1)

    every(4, groups, busy)
    every(groups, last + 1, rest)
    launch(last - 1)

    landed = goal_got.at[nx:n]
    goal_copy(1, landed, landed, (north, tx)).wait()
    goal_table = pltpu.make_async_copy(goal_got, goal_smem, local_sem.at[11])
    goal_table.start()
    goal_table.wait()

    def arrived(b, start, size):
        landed = got.at[pl.ds(start, size)]
        return pltpu.make_async_remote_copy(
            src_ref=landed, dst_ref=landed, send_sem=data_send, recv_sem=data_recv.at[b],
            device_id=(ty, east), device_id_type=MESH)

    def add(tiles, d, sums):
        sums = list(sums)
        source = lax.rem(me + (n - d) * STEP, n)
        row = lax.rem(ty + ny - lax.div(source, nx), ny) * nx + lax.rem(tx + nx - lax.rem(source, nx), nx)
        for k in range(CAP):
            tile = tiles[d, k]
            t = jnp.full((NVAR, CELLS), goal_smem[row, k], jnp.int32)
            for j in range(TBD):
                sums[j] = sums[j] + jnp.where(t == j, tile, 0.0)
        return tuple(sums)

    def collect(b, sums):
        arrived(b, b * BATCH, BATCH).wait_recv()
        return lax.fori_loop(b * BATCH, (b + 1) * BATCH, functools.partial(add, got), sums)

    zero = jnp.zeros((NVAR, CELLS), jnp.float32)
    sums = add(send, 0, (zero,) * TBD)
    arrived(0, 1, BATCH - 1).wait_recv()
    sums = lax.fori_loop(1, BATCH, functools.partial(add, got), sums)
    sums = lax.fori_loop(1, n // BATCH, collect, sums)
    arrived(0, 1, n - 1).wait_send()
    for j in range(TBD):
        out_ref[j] = sums[j] / target_area_ref[j:j + 1, :]


def on_device(
    ny, nx,
    source_fields,
    diffusivity,
    cell_area,
    pair_block,
    pair_owner,
    pair_target,
    weight_blocks,
    target_area,
):
    n = ny * nx
    nvar, rows, cols = source_fields.shape
    pairs = weight_blocks.shape[0]
    vmem = pl.BlockSpec(memory_space=pltpu.VMEM)
    hbm = pl.BlockSpec(memory_space=pltpu.HBM)
    f32, i32 = jnp.float32, jnp.int32
    tall = rows + 16
    sem = pltpu.SemaphoreType.DMA
    return pl.pallas_call(
        functools.partial(kernel, ny, nx),
        out_shape=jax.ShapeDtypeStruct((TBD, NVAR, CELLS), f32),
        in_specs=[hbm] * 8,
        out_specs=vmem,
        scratch_shapes=[
            pltpu.VMEM((2, rows, 128), f32),
            pltpu.VMEM((1, pairs), i32),
            pltpu.VMEM((1, pairs), i32),
            pltpu.VMEM((1, pairs), i32),
            pltpu.VMEM((TBD, CELLS), f32),
            pltpu.VMEM((2, 16, 128), f32),
            pltpu.VMEM((nvar, rows, cols), f32),
            pltpu.VMEM((tall * nvar, 128), f32),
            pltpu.VMEM((tall * nvar, 128), f32),
            pltpu.VMEM((tall * nvar, 128), f32),
            pltpu.VMEM((tall * nvar, 128), f32),
            pltpu.VMEM((tall * nvar, 128), f32),
            pltpu.VMEM((tall * nvar, 128), f32),
            pltpu.VMEM((3, tall, 128), f32),
            pltpu.VMEM((3, tall, 128), f32),
            pltpu.VMEM((3, tall, 128), f32),
            pltpu.VMEM((4, 8, 128), f32),
            pltpu.VMEM((8, 8, 128), f32),
            pltpu.VMEM((8, 8, 128), f32),
            pltpu.VMEM((rows // BH * BCOL, NVAR, CELLS), f32),
            pltpu.VMEM((pairs, CELLS, CELLS), jnp.bfloat16),
            pltpu.VMEM((pairs, NVAR, CELLS), f32),
            pltpu.VMEM((n, CAP, NVAR, CELLS), f32),
            pltpu.VMEM((n, CAP, NVAR, CELLS), f32),
            pltpu.VMEM((8, pairs), i32),
            pltpu.SMEM((8, pairs), i32),
            pltpu.VMEM((n, 128), i32),
            pltpu.VMEM((n, 128), i32),
            pltpu.VMEM((n, 128), i32),
            pltpu.VMEM((n, 128), i32),
            pltpu.SMEM((n, 128), i32),
            sem((12,)),
            sem((8,)),
            sem((8,)),
            sem,
            sem((n // BATCH,)),
            sem((2,)),
            sem((2,)),
            pltpu.SemaphoreType.REGULAR,
        ],
        compiler_params=pltpu.CompilerParams(
            collective_id=0, has_side_effects=True, vmem_limit_bytes=62 * 1024 * 1024),
        name="regrid",
    )(
        source_fields, diffusivity, cell_area, pair_block.reshape(1, pairs), pair_owner.reshape(1, pairs),
        pair_target.reshape(1, pairs), weight_blocks, target_area,
    )


def solution(mesh):
    return jax.shard_map(
        functools.partial(on_device, mesh.shape["ty"], mesh.shape["tx"]),
        mesh=mesh,
        in_specs=(
            P(None, "ty", "tx"),
            P("ty", "tx"),
            P("ty", "tx"),
            P(("ty", "tx")),
            P(("ty", "tx"), None),
            P(("ty", "tx")),
            P(("ty", "tx"), None, None),
            P(("ty", "tx"), None),
        ),
        out_specs=P(("ty", "tx"), None, None),
        check_vma=False,
    )
```

```python
import functools

import jax
import jax.numpy as jnp
from jax import lax
from jax.experimental import pallas as pl
from jax.experimental.pallas import tpu as pltpu
from jax.sharding import PartitionSpec as P

NVAR = 8
BH = 8
BW = 16
BR = 12
BCOL = 16
TBD = 16
CAP = 4
CELLS = BH * BW
MESH = pl.DeviceIdType.MESH
STEP, BACK = 43, 3
GROUP = 16
SLOTS = GROUP // CAP
FOLD = 32
BATCH = 8
FIRST = 14
SECOND = 2
SIDE_FIRST, SIDE_SECOND = 49, 6


def kernel(
    ny, nx,
    fields_hbm, rate_hbm, area_hbm, block_hbm, owner_hbm, target_hbm, weight_hbm, target_area_hbm,
    out_ref,
    area_ref, block_ref, owner_ref, target_ref, target_area_ref,
    area_sides, stage, x0, x1, xe, y0, y1, ye, rate, k_east, k_north, pack, from_west, from_east,
    blocks, weights, part, send, got, tables, tables_smem, goal, relay, sorted_goal, goal_got, goal_smem,
    local_sem, edge_send, edge_recv, data_send, data_recv, goal_send, goal_recv, ready,
):
    n = ny * nx
    rows, cols = rate_hbm.shape
    pairs = weight_hbm.shape[0]
    total_rows = rows * ny
    ty, tx = lax.axis_index("ty"), lax.axis_index("tx")
    me = ty * nx + tx
    north, south = lax.rem(ty + 1, ny), lax.rem(ty + ny - 1, ny)
    east, west = lax.rem(tx + 1, nx), lax.rem(tx + nx - 1, nx)
    corners = [(north, east), (north, west), (south, east), (south, west)]

    entry = pltpu.get_barrier_semaphore()
    mates = [(ty, lax.rem(tx + d, nx)) for d in range(1, nx)]
    mates += [(lax.rem(ty + d, ny), tx) for d in range(1, ny)]
    mates += corners
    for mate in mates:
        pl.semaphore_signal(entry, inc=1, device_id=mate, device_id_type=MESH)

    own = slice(8, 8 + rows)
    loads = [
        (fields_hbm, stage),
        (rate_hbm.at[:, 0:128], rate.at[0, own]),
        (rate_hbm.at[:, 128:256], rate.at[1, own]),
        (block_hbm, block_ref),
        (owner_hbm, owner_ref),
        (target_hbm, target_ref),
        (area_hbm.at[:, 0:128], area_ref.at[0]),
        (area_hbm.at[:, 128:256], area_ref.at[1]),
        (target_area_hbm, target_area_ref),
        (weight_hbm, weights),
    ]
    loads = [pltpu.make_async_copy(src, dst, local_sem.at[i]) for i, (src, dst) in enumerate(loads)]
    for load in loads[:-1]:
        load.start()
    for load in loads[:3]:
        load.wait()
    loads[-1].start()

    lane = lax.broadcasted_iota(jnp.int32, (8, 128), 1)
    xs, ys = (x0, x1), (y0, y1)

    def row(field, r):
        return field[pl.ds(pl.multiple_of(r * NVAR, NVAR), NVAR), :]

    def turn(i, carry):
        for v in range(NVAR):
            for t in range(2):
                tile = stage[v, pl.ds(pl.multiple_of(8 * i, 8), 8), 128 * t:128 * t + 128]
                xs[t][pl.ds((8 + 8 * i) * NVAR + v, 8, stride=NVAR), :] = tile
        return carry

    lax.fori_loop(0, rows // 8, turn, 0)

    def packed(firsts, lasts):
        total = jnp.zeros((8, 128), jnp.float32)
        for j, (first, last) in enumerate(zip(firsts, lasts)):
            edge = pltpu.roll(jnp.where(lane < 64, first, last), 4 * j + 2, 1)
            total = jnp.where((lane >= 4 * j) & (lane < 4 * j + 4), edge, total)
        return total

    for g, place in enumerate((0, 3, 2)):
        group = range(8 + FOLD * g, 8 + FOLD * (g + 1))
        pack[place] = packed([row(x0, r) for r in group], [row(x1, r) for r in group])
    group = range(8, 8 + rows, 8)
    pack[1] = packed([rate[0, r:r + 8, :] for r in group], [rate[1, r:r + 8, :] for r in group])

    pl.semaphore_wait(entry, len(mates))

    def edge_copy(i, src, dst, device):
        return pltpu.make_async_remote_copy(
            src_ref=src, dst_ref=dst, send_sem=edge_send.at[i], recv_sem=edge_recv.at[i],
            device_id=device, device_id_type=MESH)

    low, high = slice(6 * NVAR, 8 * NVAR), slice((8 + rows) * NVAR, (10 + rows) * NVAR)
    top, bottom = slice((6 + rows) * NVAR, (8 + rows) * NVAR), slice(8 * NVAR, 10 * NVAR)
    rate_low, rate_high = rate.at[0:2, 0:8], rate.at[0:2, 8 + rows:16 + rows]
    edges = [
        (0, pack.at[1:3], from_west.at[4:6], corners[0]),
        (1, pack.at[1:3], from_east.at[4:6], corners[1]),
        (0, pack.at[0:2], from_west.at[6:8], corners[2]),
        (1, pack.at[0:2], from_east.at[6:8], corners[3]),
        (0, pack, from_west.at[0:4], (ty, east)),
        (1, pack, from_east.at[0:4], (ty, west)),
        (2, x0.at[top], x0.at[low], (north, tx)),
        (3, x1.at[top], x1.at[low], (north, tx)),
        (4, rate.at[0:2, rows:8 + rows], rate_low, (north, tx)),
        (5, x0.at[bottom], x0.at[high], (south, tx)),
        (6, x1.at[bottom], x1.at[high], (south, tx)),
        (7, rate.at[0:2, 8:16], rate_high, (south, tx)),
    ]
    for edge in edges:
        edge_copy(*edge).start()
    for d in range(1, ny):
        pl.semaphore_signal(ready, inc=1, device_id=(lax.rem(ty + d, ny), tx), device_id_type=MESH)

    for load in loads[3:6]:
        load.wait()
    p_lane = lax.broadcasted_iota(jnp.int32, (1, pairs), 1)
    p_row = lax.broadcasted_iota(jnp.int32, (pairs, 1), 0)
    key_row = jnp.bitwise_and((owner_ref[...] - me + n) * BACK, n - 1)
    joint_row = p_lane * 4096 + block_ref[...] * TBD + target_ref[...]
    goal_row = target_ref[...] + 1
    eye = lax.broadcasted_iota(jnp.int32, (pairs, pairs), 0) == lax.broadcasted_iota(jnp.int32, (pairs, pairs), 1)

    def along(axis, mask, value):
        return jnp.sum(jnp.where(mask, value, 0), axis=axis, keepdims=True, dtype=jnp.int32)

    unique_row = key_row * pairs + p_lane
    key_col = along(1, eye, key_row)
    joint_col = along(1, eye, joint_row)
    unique_col = key_col * pairs + p_row
    place_row = along(0, unique_col < unique_row, 1)
    place_col = along(1, unique_row < unique_col, 1)
    joint = along(0, place_col == p_lane, joint_col)
    tables[0:1, :] = jnp.clip(lax.shift_right_logical(joint, 12), 0, pairs - 1)
    tables[1:2, :] = jnp.clip(jnp.bitwise_and(lax.shift_right_logical(joint, 4), 255), 0, blocks.shape[0] - 1)
    tables[2:3, :] = along(0, key_col < p_lane, 1)
    table_copy = pltpu.make_async_copy(tables, tables_smem, local_sem.at[10])
    table_copy.start()

    r_col = lax.broadcasted_iota(jnp.int32, (n, 1), 0)
    owner_col = lax.rem(r_col, ny) * nx + lax.div(r_col, ny)
    d_col = jnp.bitwise_and((owner_col - me + n) * BACK, n - 1)
    rank = jnp.where(key_row == d_col, place_row - along(1, key_row < d_col, 1), -1)
    d_lane = lax.broadcasted_iota(jnp.int32, (n, 128), 1)
    goals = jnp.zeros((n, 128), jnp.int32)
    for k in range(CAP):
        goals = jnp.where(d_lane == k, along(1, rank == k, goal_row), goals)
    goal[...] = goals - 1

    def rows_of(i, size):
        return pl.ds(pl.multiple_of(i * size, 8), size)

    def goal_copy(i, src, dst, device):
        return pltpu.make_async_remote_copy(
            src_ref=src, dst_ref=dst, send_sem=goal_send.at[i], recv_sem=goal_recv.at[i],
            device_id=device, device_id_type=MESH)

    along_tx, along_ty = [], []
    for d in range(1, nx):
        to = lax.rem(tx + d, nx)
        along_tx.append(goal_copy(0, goal.at[rows_of(to, ny)], relay.at[d * ny:(d + 1) * ny], (ty, to)))
    for d in range(1, ny):
        to = lax.rem(ty + d, ny)
        along_ty.append(goal_copy(1, sorted_goal.at[rows_of(to, nx)], goal_got.at[d * nx:(d + 1) * nx], (to, tx)))
    for copy in along_tx:
        copy.start()
    relay[0:ny, :] = goal[rows_of(tx, ny), :]

    sub = lax.broadcasted_iota(jnp.int32, (8, 128), 0)
    inner = (rows + 8) // 8
    bands = inner + 1

    def from_next(tiles):
        moved = [pltpu.roll(c, 127, 1) for c in tiles]
        if len(tiles) == 1:
            return moved
        return [jnp.where(lane < 127, moved[t], moved[1 - t]) for t in range(2)]

    def from_previous(tiles):
        moved = [pltpu.roll(c, 1, 1) for c in tiles]
        if len(tiles) == 1:
            return moved
        return [jnp.where(lane > 0, moved[t], moved[1 - t]) for t in range(2)]

    def rate_band(tiles, i, last):
        here, above = [[rate[t, 8 * b:8 * b + 8, :] for t in tiles] for b in (i, min(i + 1, last))]
        g = sub + (ty * rows + 8 * i - 8)
        inside = (g >= 0) & (g < total_rows - 1)
        for t, c, n_value, e in zip(tiles, here, above, from_next(here)):
            n_value = jnp.where(sub < 7, pltpu.roll(c, 7, 0), pltpu.roll(n_value, 7, 0))
            k_east[t, 8 * i:8 * i + 8, :] = 0.5 * (c + e)
            k_north[t, 8 * i:8 * i + 8, :] = jnp.where(inside, 0.5 * (c + n_value), 0.0)

    def north_flux(t, r, c, n_value):
        return k_north[t, pl.ds(r, 1), :] * (n_value - c)

    def advance(fields, tiles, r, c, below):
        above = [row(field, r + 1) for field in fields]
        flux = [north_flux(t, r, *pair) for t, pair in zip(tiles, zip(c, above))]
        side = [k_east[t, pl.ds(r, 1), :] * (e - p) for t, p, e in zip(tiles, c, from_next(c))]
        back = from_previous(side)
        return above, flux, [p + a - b + f - q for p, a, b, f, q in zip(c, side, back, flux, below)]

    def begin_at(fields, tiles, r):
        c = [row(field, r) for field in fields]
        return c, [north_flux(t, r - 1, row(field, r - 1), p) for t, field, p in zip(tiles, fields, c)]

    def first_pass(fields, results, tiles, start, count, carry):
        for u in range(count):
            *carry, z = advance(fields, tiles, start + u, *carry)
            for result, p in zip(results, z):
                result[pl.ds(pl.multiple_of((start + u) * NVAR, NVAR), NVAR), :] = p
        return tuple(carry)

    def second_pass(fields, tiles, block, carry):
        out = []
        for j in range(BH):
            *carry, z = advance(fields, tiles, 8 + block * BH + j, *carry)
            out.append(z)
        return tuple(carry), out

    def whole_blocks(block, carry):
        carry, out = second_pass(ys, (0, 1), block, carry)
        for t in range(2):
            tile = [area_ref[t, pl.ds(block * BH + j, 1), :] * z[t] for j, z in enumerate(out)]
            for bit in (1, 2, 4):
                mask = jnp.bitwise_and(lane, 16 * bit) == 0
                for j in range(BH):
                    if j & bit:
                        continue
                    lo, hi = tile[j], tile[j + bit]
                    tile[j] = jnp.where(mask, lo, pltpu.roll(hi, 16 * bit, 1))
                    tile[j + bit] = jnp.where(mask, pltpu.roll(lo, 128 - 16 * bit, 1), hi)
            for j in range(BH):
                blocks[block * BCOL + t * BH + j] = tile[j]
        return carry

    for i in range(1, inner):
        rate_band((0, 1), i, inner - 1)
    block_rows = rows // BH
    every_row = lambda r: jnp.where(lane < 60, row(x0, r), pltpu.roll(row(x1, r), 124, 1))

    def inside_first(b, carry):
        for u in range(FIRST):
            r = 14 + b * FIRST + u
            xe[pl.ds(pl.multiple_of(r * NVAR, NVAR), NVAR), :] = every_row(r)
        return first_pass(xs, ys, (0, 1), 14 + b * FIRST, FIRST, carry)

    lax.fori_loop(0, (rows - 12) // FIRST, inside_first, begin_at(xs, (0, 1), 14))
    for load in loads[6:8]:
        load.wait()

    def inside_second(b, carry):
        for u in range(SECOND):
            carry = whole_blocks(1 + b * SECOND + u, carry)
        return carry

    lax.fori_loop(0, (block_rows - 2) // SECOND, inside_second, begin_at(ys, (0, 1), 16))

    for block in range(block_rows):
        for t, base in enumerate((0, 112)):
            total = jnp.zeros((1, 128), jnp.float32)
            for j in range(BH):
                moved = pltpu.roll(jnp.broadcast_to(area_ref[t, block * BH + j:block * BH + j + 1, :], (8, 128)), (16 * j - base) % 128, 1)
                total = jnp.where(lax.shift_right_logical(lane[0:1], 4) == j, moved[0:1], total)
            area_sides[t, block:block + 1, :] = total

    landing = (from_west, from_east, x0.at[low], x1.at[low], rate_low, x0.at[high], x1.at[high], rate_high)
    for i, landed in enumerate(landing):
        edge_copy(i, landed, landed, (ty, east)).wait()

    for i in (0, inner - 1, inner):
        rate_band((0, 1), i, inner)

    def ends(side, carry):
        start = 7 + side * (rows - 5)
        first_pass(xs, ys, (0, 1), start, 7, begin_at(xs, (0, 1), start))
        return carry

    ends(0, 0)
    ends(1, 0)

    def end_blocks(side, carry):
        block = side * (block_rows - 1)
        whole_blocks(block, begin_at(ys, (0, 1), 8 + block * BH))
        return carry

    end_blocks(0, 0)
    end_blocks(1, 0)

    both = []
    for i in range(8):
        both.append(jnp.where(jnp.bitwise_and(lane, 3) < 2, pltpu.roll(from_east[i], 126, 1), pltpu.roll(from_west[i], 2, 1)))

    def opened(tile, j):
        return pltpu.roll(tile, 124 - 4 * j, 1) if j < 31 else tile

    def put(r, tile, j):
        own_part = xe[NVAR * r:NVAR * r + NVAR, :] if 14 <= r < 2 + rows else every_row(r)
        xe[NVAR * r:NVAR * r + NVAR, :] = jnp.where(lane < 124, own_part, opened(tile, j))

    for g, place in enumerate((0, 3, 2)):
        for j in range(FOLD):
            put(8 + FOLD * g + j, both[place], j)
    put(7, both[5], FOLD - 1)
    put(8 + rows, both[6], 0)
    for r in (6, 9 + rows):
        xe[NVAR * r:NVAR * r + NVAR, :] = every_row(r)
    for i in range(bands):
        if i == 0:
            side = opened(both[4], rows // 8 - 1)
        elif i == inner:
            side = opened(both[7], 0)
        else:
            side = opened(both[1], i - 1)
        own_part = jnp.where(lane < 60, rate[0, 8 * i:8 * i + 8, :], pltpu.roll(rate[1, 8 * i:8 * i + 8, :], 124, 1))
        rate[2, 8 * i:8 * i + 8, :] = jnp.where(lane < 124, own_part, side)
    for i in range(bands):
        rate_band((2,), i, inner)

    def side_first(b, carry):
        return first_pass((xe,), (ye,), (2,), 7 + b * SIDE_FIRST, SIDE_FIRST, carry)

    lax.fori_loop(0, (rows + 2) // SIDE_FIRST, side_first, begin_at((xe,), (2,), 7))

    def side_second(b, carry):
        for u in range(SIDE_SECOND):
            block = b * SIDE_SECOND + u
            carry, out = second_pass((ye,), (2,), block, carry)
            left, right = None, None
            for j, (z,) in enumerate(out):
                l_value = pltpu.roll(z, 16 * j, 1) if j else z
                r_value = pltpu.roll(z, (16 * j + 20) % 128, 1)
                here = lax.shift_right_logical(lane, 4) == j
                left = l_value if j == 0 else jnp.where(here, l_value, left)
                right = r_value if j == 0 else jnp.where(here, r_value, right)
            blocks[block * BCOL] = left * area_sides[0, pl.ds(block, 1), :]
            blocks[block * BCOL + BCOL - 1] = right * area_sides[1, pl.ds(block, 1), :]
        return carry

    lax.fori_loop(0, block_rows // SIDE_SECOND, side_second, begin_at((ye,), (2,), 8))

    def peer(d):
        p = lax.rem(me + lax.rem(d * STEP, n), n)
        return (p // nx, lax.rem(p, nx))

    def data_copy(d):
        return pltpu.make_async_remote_copy(
            src_ref=send.at[d], dst_ref=got.at[d], send_sem=data_send,
            recv_sem=data_recv.at[lax.div(d, BATCH)], device_id=peer(d), device_id_type=MESH)

    def every(start, stop, action):
        def body(d, carry):
            action(d)
            return carry
        lax.fori_loop(start, stop, body, 0)

    table_copy.wait()
    for load in loads[8:]:
        load.wait()

    def multiply(q):
        for u in range(GROUP):
            i = q * GROUP + u
            a = blocks[tables_smem[1, i]].astype(jnp.bfloat16)
            part[i] = jnp.dot(a, weights[tables_smem[0, i]], preferred_element_type=jnp.float32)

    def fill(q):
        for u in range(SLOTS):
            d = q * SLOTS + u
            first = tables_smem[2, d]
            for k in range(CAP):
                send[d, k] = part[jnp.minimum(first + k, pairs - 1)]

    def launch(q):
        for u in range(SLOTS):
            data_copy(q * SLOTS + u).start()

    last = n // SLOTS
    groups = pairs // GROUP
    multiply(0)
    fill(0)
    multiply(1)
    pl.semaphore_wait(ready, ny - 1)
    for u in range(1, SLOTS):
        data_copy(u).start()
    fill(1)
    multiply(2)

    landed = relay.at[ny:n]
    goal_copy(0, landed, landed, (ty, east)).wait()
    for i in range(ny):
        sorted_goal[i * nx:(i + 1) * nx, :] = relay[pl.ds(i, nx, stride=ny), :]
    goal_got[0:nx, :] = sorted_goal[rows_of(ty, nx), :]
    launch(1)
    fill(2)
    multiply(3)
    for copy in along_ty:
        copy.start()

    def busy(q):
        launch(q - 2)
        fill(q - 1)
        multiply(q)

    def rest(q):
        launch(q - 2)
        fill(q - 1)

    every(4, groups, busy)
    every(groups, last + 1, rest)
    launch(last - 1)

    landed = goal_got.at[nx:n]
    goal_copy(1, landed, landed, (north, tx)).wait()
    goal_table = pltpu.make_async_copy(goal_got, goal_smem, local_sem.at[11])
    goal_table.start()
    goal_table.wait()

    def arrived(b, start, size):
        landed = got.at[pl.ds(start, size)]
        return pltpu.make_async_remote_copy(
            src_ref=landed, dst_ref=landed, send_sem=data_send, recv_sem=data_recv.at[b],
            device_id=(ty, east), device_id_type=MESH)

    def add(tiles, d, sums):
        sums = list(sums)
        source = lax.rem(me + (n - d) * STEP, n)
        row = lax.rem(ty + ny - lax.div(source, nx), ny) * nx + lax.rem(tx + nx - lax.rem(source, nx), nx)
        for k in range(CAP):
            tile = tiles[d, k]
            t = jnp.full((NVAR, CELLS), goal_smem[row, k], jnp.int32)
            for j in range(TBD):
                sums[j] = sums[j] + jnp.where(t == j, tile, 0.0)
        return tuple(sums)

    def collect(b, sums):
        arrived(b, b * BATCH, BATCH).wait_recv()
        return lax.fori_loop(b * BATCH, (b + 1) * BATCH, functools.partial(add, got), sums)

    zero = jnp.zeros((NVAR, CELLS), jnp.float32)
    sums = add(send, 0, (zero,) * TBD)
    arrived(0, 1, BATCH - 1).wait_recv()
    sums = lax.fori_loop(1, BATCH, functools.partial(add, got), sums)
    sums = lax.fori_loop(1, n // BATCH, collect, sums)
    arrived(0, 1, n - 1).wait_send()
    for j in range(TBD):
        out_ref[j] = sums[j] / target_area_ref[j:j + 1, :]


def on_device(
    ny, nx,
    source_fields,
    diffusivity,
    cell_area,
    pair_block,
    pair_owner,
    pair_target,
    weight_blocks,
    target_area,
):
    n = ny * nx
    nvar, rows, cols = source_fields.shape
    pairs = weight_blocks.shape[0]
    vmem = pl.BlockSpec(memory_space=pltpu.VMEM)
    hbm = pl.BlockSpec(memory_space=pltpu.HBM)
    f32, i32 = jnp.float32, jnp.int32
    tall = rows + 16
    sem = pltpu.SemaphoreType.DMA
    return pl.pallas_call(
        functools.partial(kernel, ny, nx),
        out_shape=jax.ShapeDtypeStruct((TBD, NVAR, CELLS), f32),
        in_specs=[hbm] * 8,
        out_specs=vmem,
        scratch_shapes=[
            pltpu.VMEM((2, rows, 128), f32),
            pltpu.VMEM((1, pairs), i32),
            pltpu.VMEM((1, pairs), i32),
            pltpu.VMEM((1, pairs), i32),
            pltpu.VMEM((TBD, CELLS), f32),
            pltpu.VMEM((2, 16, 128), f32),
            pltpu.VMEM((nvar, rows, cols), f32),
            pltpu.VMEM((tall * nvar, 128), f32),
            pltpu.VMEM((tall * nvar, 128), f32),
            pltpu.VMEM((tall * nvar, 128), f32),
            pltpu.VMEM((tall * nvar, 128), f32),
            pltpu.VMEM((tall * nvar, 128), f32),
            pltpu.VMEM((tall * nvar, 128), f32),
            pltpu.VMEM((3, tall, 128), f32),
            pltpu.VMEM((3, tall, 128), f32),
            pltpu.VMEM((3, tall, 128), f32),
            pltpu.VMEM((4, 8, 128), f32),
            pltpu.VMEM((8, 8, 128), f32),
            pltpu.VMEM((8, 8, 128), f32),
            pltpu.VMEM((rows // BH * BCOL, NVAR, CELLS), f32),
            pltpu.VMEM((pairs, CELLS, CELLS), jnp.bfloat16),
            pltpu.VMEM((pairs, NVAR, CELLS), f32),
            pltpu.VMEM((n, CAP, NVAR, CELLS), f32),
            pltpu.VMEM((n, CAP, NVAR, CELLS), f32),
            pltpu.VMEM((8, pairs), i32),
            pltpu.SMEM((8, pairs), i32),
            pltpu.VMEM((n, 128), i32),
            pltpu.VMEM((n, 128), i32),
            pltpu.VMEM((n, 128), i32),
            pltpu.VMEM((n, 128), i32),
            pltpu.SMEM((n, 128), i32),
            sem((12,)),
            sem((8,)),
            sem((8,)),
            sem,
            sem((n // BATCH,)),
            sem((2,)),
            sem((2,)),
            pltpu.SemaphoreType.REGULAR,
        ],
        compiler_params=pltpu.CompilerParams(
            collective_id=0, has_side_effects=True, vmem_limit_bytes=62 * 1024 * 1024),
        name="regrid",
    )(
        source_fields, diffusivity, cell_area, pair_block.reshape(1, pairs), pair_owner.reshape(1, pairs),
        pair_target.reshape(1, pairs), weight_blocks, target_area,
    )


def solution(mesh):
    return jax.shard_map(
        functools.partial(on_device, mesh.shape["ty"], mesh.shape["tx"]),
        mesh=mesh,
        in_specs=(
            P(None, "ty", "tx"),
            P("ty", "tx"),
            P("ty", "tx"),
            P(("ty", "tx")),
            P(("ty", "tx"), None),
            P(("ty", "tx")),
            P(("ty", "tx"), None, None),
            P(("ty", "tx"), None),
        ),
        out_specs=P(("ty", "tx"), None, None),
        check_vma=False,
    )
```
